32 devices in a mesh: dp: 4 (over x, core), space: 8 (over z, y).
Axes of the slice: x: 2, y: 2, z: 4, core: 2. Of those that a mesh axis runs over, the one named last changes fastest.
Arguments:
- features: bfloat16 [4, 512, 32768], P('dp', 'space'), may hold values from -6 to 6
- cotangent: bfloat16 [4, 512, 32768], P('dp', 'space'), may hold values from -6 to 6
- spec_weight: bfloat16 [2, 32, 64, 64], replicated, may hold values from -0.5 to 0.5
- skip_weight: bfloat16 [64, 64], replicated, may hold values from -0.75 to 0.75
- w_in: bfloat16 [64, 256], replicated, may hold values from -0.75 to 0.75
- w_out: bfloat16 [256, 64], replicated, may hold values from -0.375 to 0.375
Outputs:
- mixed: bfloat16 [4, 512, 32768], P('dp', 'space')
- grad_features: bfloat16 [4, 512, 32768], P('dp', 'space')
- grad_spec: float32 [2, 32, 64, 64], replicated
- grad_skip: float32 [64, 64], replicated
- grad_in: float32 [64, 256], replicated
- grad_out: float32 [256, 64], replicated
The draws below stay inside these ranges and needn't reach their ends.
All inputs are finite; a program needn't handle non-finite values.
Results may differ from the reference program's by a relative error of at most 0.0084.
Values may be sent and summed in bfloat16 or wider, within the bound.
No kernel may reach another device: no remote copies, remote signals or barrier semaphores. Data moves between devices by JAX's collectives and lax.ppermute only.
A program may use at most 192 MiB of HBM per device.

```python
import math
import jax
import jax.numpy as jnp
from jax import lax

NX = 512
C = 64
M = 32
F = 256
P_SIZE = 512
BATCH = 4


def levels(key, shape, shards, smallest, high):
    loudness = 1.0
    for axis_at, shards_of in shards:
        draws = jax.random.uniform(jax.random.fold_in(jax.random.fold_in(key, 6), axis_at), (shards_of,), jnp.float32, smallest / len(shards), high / len(shards))
        loudness = loudness * jnp.repeat(jnp.exp(draws), shape[axis_at] // shards_of).reshape((-1,) + (1,) * (len(shape) - 1 - axis_at))
    return loudness


def gaussian(own_key, dims, width, reach, shards=(), kind=jnp.bfloat16):
    values = width * jax.random.normal(own_key, dims, jnp.float32)
    if shards:
        values = values * levels(own_key, dims, shards, -0.22, 0.18)
    return jnp.clip(values, -reach, reach).astype(kind)


def setup_inputs(seed: int = 0) -> dict:
    arg_keys = jax.random.split(jax.random.key(seed), 7)
    features = gaussian(arg_keys[0], (BATCH, NX, P_SIZE * C), 1.0, 6.0, ((0, 4), (1, 8)))
    cotangent = gaussian(arg_keys[1], (BATCH, NX, P_SIZE * C), 1.0, 6.0, ((0, 4), (1, 8)))
    spec_weight = gaussian(arg_keys[2], (2, M, C, C), (2 * C) ** -0.5, 0.5)
    skip_weight = gaussian(arg_keys[3], (C, C), C ** -0.5, 0.75)
    w_in = gaussian(arg_keys[4], (C, F), C ** -0.5, 0.75)
    w_out = gaussian(arg_keys[5], (F, C), F ** -0.5, 0.375)
    return {"features": features, "cotangent": cotangent, "spec_weight": spec_weight, "skip_weight": skip_weight, "w_in": w_in, "w_out": w_out}


gelu_scale = math.sqrt(2.0 / math.pi)
gelu_cubic = 0.044715

def gelu_tanh(values):
    inner = jnp.tanh(gelu_scale * (values + gelu_cubic * values * values * values))
    return 0.5 * values * (1.0 + inner)

def gelu_slope(values):
    inner = jnp.tanh(gelu_scale * (values + gelu_cubic * values * values * values))
    return 0.5 * (1.0 + inner) + 0.5 * values * (1.0 - inner * inner) * gelu_scale * (1.0 + 3.0 * gelu_cubic * values * values)

def dft_tables(length, modes, first, count):
    places = first + jnp.arange(count, dtype=jnp.int32)
    freqs = jnp.arange(modes, dtype=jnp.int32)
    phase = (freqs[:, None] * places[None, :] % length).astype(jnp.float32) * (2.0 * math.pi / length)
    cosine = jnp.cos(phase)
    sine = jnp.sin(phase)
    forward_tab = jnp.concatenate([cosine, -sine], 0).astype(jnp.bfloat16)
    factor = jnp.where(freqs == 0, 1.0, 2.0).astype(jnp.float32)[:, None] / length
    inverse_tab = jnp.concatenate([factor * cosine, -factor * sine], 0).T.astype(jnp.bfloat16)
    return (forward_tab, inverse_tab)

def wide_einsum(form, left, right):
    return jnp.einsum(form, left.astype(jnp.float32), right.astype(jnp.float32))

def layer_block(fields, cotan, spec_weight, skip_weight, w_in, w_out, forward_tab, inverse_tab):
    spectrum = wide_einsum('kx,xpc->kpc', forward_tab, fields).astype(jnp.bfloat16)
    real_part = spectrum[:M]
    imag_part = spectrum[M:]
    weight_real = spec_weight[0]
    weight_imag = spec_weight[1]
    out_real = wide_einsum('mpc,moc->mpo', real_part, weight_real) - wide_einsum('mpc,moc->mpo', imag_part, weight_imag)
    out_imag = wide_einsum('mpc,moc->mpo', imag_part, weight_real) + wide_einsum('mpc,moc->mpo', real_part, weight_imag)
    modal = jnp.concatenate([out_real, out_imag], 0).astype(jnp.bfloat16)
    spatial = lax.optimization_barrier(wide_einsum('xk,kpo->xpo', inverse_tab, modal).astype(jnp.bfloat16))
    preact = spatial.astype(jnp.float32) + wide_einsum('xpc,oc->xpo', fields, skip_weight)
    activated = gelu_tanh(preact).astype(jnp.bfloat16)
    inner = wide_einsum('xpc,cf->xpf', activated, w_in)
    hidden = gelu_tanh(inner).astype(jnp.bfloat16)
    mixed = wide_einsum('xpf,fc->xpc', hidden, w_out).astype(jnp.bfloat16)
    grad_inner = (wide_einsum('xpc,fc->xpf', cotan, w_out) * gelu_slope(inner)).astype(jnp.bfloat16)
    grad_out = wide_einsum('xpf,xpc->fc', hidden, cotan)
    grad_in = wide_einsum('xpc,xpf->cf', activated, grad_inner)
    grad_pre = (wide_einsum('xpf,cf->xpc', grad_inner, w_in) * gelu_slope(preact)).astype(jnp.bfloat16)
    grad_skip = wide_einsum('xpo,xpc->oc', grad_pre, fields)
    grad_modal = wide_einsum('xk,xpo->kpo', inverse_tab, grad_pre).astype(jnp.bfloat16)
    grad_real = grad_modal[:M]
    grad_imag = grad_modal[M:]
    spec_real = wide_einsum('mpo,mpc->moc', grad_real, real_part) + wide_einsum('mpo,mpc->moc', grad_imag, imag_part)
    spec_imag = wide_einsum('mpo,mpc->moc', grad_imag, real_part) - wide_einsum('mpo,mpc->moc', grad_real, imag_part)
    back_real = wide_einsum('moc,mpo->mpc', weight_real, grad_real) + wide_einsum('moc,mpo->mpc', weight_imag, grad_imag)
    back_imag = wide_einsum('moc,mpo->mpc', weight_real, grad_imag) - wide_einsum('moc,mpo->mpc', weight_imag, grad_real)
    grad_spectrum = jnp.concatenate([back_real, back_imag], 0).astype(jnp.bfloat16)
    grad_fields = (wide_einsum('kx,kpc->xpc', forward_tab, grad_spectrum) + wide_einsum('xpo,oc->xpc', grad_pre, skip_weight)).astype(jnp.bfloat16)
    grad_spec = jnp.stack([spec_real, spec_imag], 0)
    return (mixed, grad_fields, grad_spec, grad_skip, grad_in, grad_out)

def reference(features, cotangent, spec_weight, skip_weight, w_in, w_out):
    block_width = min(P_SIZE, 256)
    block_count = P_SIZE // block_width

    def split_blocks(array):
        return array.reshape(BATCH, NX, block_count, block_width, C).transpose(0, 2, 1, 3, 4).reshape(BATCH * block_count, NX, block_width, C)

    def merge_blocks(array):
        return array.reshape(BATCH, block_count, NX, block_width, C).transpose(0, 2, 1, 3, 4).reshape(BATCH, NX, P_SIZE * C)
    forward_tab, inverse_tab = dft_tables(NX, M, 0, NX)
    initial = (jnp.zeros((2, M, C, C), jnp.float32), jnp.zeros((C, C), jnp.float32), jnp.zeros((C, F), jnp.float32), jnp.zeros((F, C), jnp.float32))

    def advance(carry, pair):
        results = layer_block(pair[0], pair[1], spec_weight, skip_weight, w_in, w_out, forward_tab, inverse_tab)
        totals = tuple((total + part for total, part in zip(carry, results[2:])))
        return (totals, (results[0], results[1]))
    totals, outputs = lax.scan(advance, initial, (split_blocks(features), split_blocks(cotangent)))
    return (merge_blocks(outputs[0]), merge_blocks(outputs[1]), totals[0], totals[1], totals[2], totals[3])
```

```python
import functools
import math

import jax
import jax.numpy as jnp
import ml_dtypes
import numpy as np
from jax import lax
from jax.experimental import pallas as pl
from jax.experimental.pallas import tpu as pltpu
from jax.sharding import PartitionSpec as P

gelu_scale = math.sqrt(2.0 / math.pi)
gelu_cubic = 0.044715
half = jnp.bfloat16
full = jnp.float32
chunks = 4
lanes = 128


def gelu_tanh(values):
    inner = jnp.tanh(gelu_scale * (values + gelu_cubic * values * values * values))
    return 0.5 * values * (1.0 + inner)


def gelu_slope(values):
    inner = jnp.tanh(gelu_scale * (values + gelu_cubic * values * values * values))
    return 0.5 * (1.0 + inner) + 0.5 * values * (1.0 - inner * inner) * gelu_scale * (
        1.0 + 3.0 * gelu_cubic * values * values
    )


def dft_tables(length, modes):
    places = np.arange(length)
    freqs = np.arange(modes)
    phase = (freqs[:, None] * places[None, :] % length).astype(np.float32) * np.float32(
        2.0 * math.pi / length
    )
    cosine = np.cos(phase).astype(np.float32)
    sine = np.sin(phase).astype(np.float32)
    forward_tab = np.concatenate([cosine, -sine], 0).astype(ml_dtypes.bfloat16)
    factor = np.where(freqs == 0, 1.0, 2.0).astype(np.float32)[:, None] / np.float32(length)
    inverse_tab = np.concatenate([factor * cosine, -factor * sine], 0).T.astype(ml_dtypes.bfloat16)
    return forward_tab, inverse_tab


def contract(form, left, right):
    return jnp.einsum(form, left, right, preferred_element_type=full)


def spectral_forward(fields, forward_tab, inverse_tab, spec_weight):
    modes = spec_weight.shape[1]
    spectrum = contract("kx,bxpc->bkpc", forward_tab, fields).astype(half)
    real_part = spectrum[:, :modes]
    imag_part = spectrum[:, modes:]
    weight_real = spec_weight[0]
    weight_imag = spec_weight[1]
    out_real = contract("bmpc,moc->bmpo", real_part, weight_real) - contract(
        "bmpc,moc->bmpo", imag_part, weight_imag
    )
    out_imag = contract("bmpc,moc->bmpo", imag_part, weight_real) + contract(
        "bmpc,moc->bmpo", real_part, weight_imag
    )
    modal = jnp.concatenate([out_real, out_imag], 1).astype(half)
    spatial = lax.optimization_barrier(contract("xk,bkpo->bxpo", inverse_tab, modal).astype(half))
    return spectrum, spatial


def pointwise(fields, spatial, cotan, skip_weight, w_in, w_out):
    preact = spatial.astype(full) + contract("bxpc,oc->bxpo", fields, skip_weight)
    activated = gelu_tanh(preact).astype(half)
    inner = contract("bxpc,cf->bxpf", activated, w_in)
    hidden = gelu_tanh(inner).astype(half)
    mixed = contract("bxpf,fc->bxpc", hidden, w_out).astype(half)
    grad_inner = (contract("bxpc,fc->bxpf", cotan, w_out) * gelu_slope(inner)).astype(half)
    grad_out = contract("bxpf,bxpc->fc", hidden, cotan)
    grad_in = contract("bxpc,bxpf->cf", activated, grad_inner)
    grad_pre = (contract("bxpf,cf->bxpc", grad_inner, w_in) * gelu_slope(preact)).astype(half)
    grad_skip = contract("bxpo,bxpc->oc", grad_pre, fields)
    return mixed, grad_pre, (grad_skip, grad_in, grad_out)


def spectral_backward(spectrum, grad_pre, forward_tab, inverse_tab, spec_weight, skip_weight):
    modes = spec_weight.shape[1]
    real_part = spectrum[:, :modes]
    imag_part = spectrum[:, modes:]
    weight_real = spec_weight[0]
    weight_imag = spec_weight[1]
    grad_modal = contract("xk,bxpo->bkpo", inverse_tab, grad_pre).astype(half)
    grad_real = grad_modal[:, :modes]
    grad_imag = grad_modal[:, modes:]
    spec_real = contract("bmpo,bmpc->moc", grad_real, real_part) + contract(
        "bmpo,bmpc->moc", grad_imag, imag_part
    )
    spec_imag = contract("bmpo,bmpc->moc", grad_imag, real_part) - contract(
        "bmpo,bmpc->moc", grad_real, imag_part
    )
    back_real = contract("moc,bmpo->bmpc", weight_real, grad_real) + contract(
        "moc,bmpo->bmpc", weight_imag, grad_imag
    )
    back_imag = contract("moc,bmpo->bmpc", weight_real, grad_imag) - contract(
        "moc,bmpo->bmpc", weight_imag, grad_real
    )
    grad_spectrum = jnp.concatenate([back_real, back_imag], 1).astype(half)
    grad_fields = (
        contract("kx,bkpc->bxpc", forward_tab, grad_spectrum)
        + contract("bxpo,oc->bxpc", grad_pre, skip_weight)
    ).astype(half)
    return jnp.stack([spec_real, spec_imag], 0), grad_fields


def pencil_shards(features, cotangent, spec_weight, skip_weight, w_in, w_out):
    span = lax.axis_size("space")
    batch, slab, flat = features.shape
    width = skip_weight.shape[0]
    modes = spec_weight.shape[1]
    length = slab * span
    positions = flat // width
    columns = positions // span
    forward_tab, inverse_tab = (jnp.asarray(table) for table in dft_tables(length, modes))
    pencil_shape = (batch, length, columns, width)
    pencil_flat = (batch, length, columns * width)
    pencil_u = lax.all_to_all(features, "space", split_axis=2, concat_axis=1, tiled=True)
    spectrum, spatial = spectral_forward(
        pencil_u.reshape(pencil_shape), forward_tab, inverse_tab, spec_weight
    )
    spatial_slab = lax.all_to_all(
        spatial.reshape(pencil_flat), "space", split_axis=1, concat_axis=2, tiled=True
    )
    slab_shape = (batch, slab, positions, width)
    mixed_four, grad_pre, mlp_grads = pointwise(
        features.reshape(slab_shape),
        spatial_slab.reshape(slab_shape),
        cotangent.reshape(slab_shape),
        skip_weight,
        w_in,
        w_out,
    )
    pencil_grad = lax.all_to_all(
        grad_pre.reshape(batch, slab, flat), "space", split_axis=2, concat_axis=1, tiled=True
    )
    grad_spec, grad_pencil = spectral_backward(
        spectrum,
        pencil_grad.reshape(pencil_shape),
        forward_tab,
        inverse_tab,
        spec_weight,
        skip_weight,
    )
    grad_fields = lax.all_to_all(
        grad_pencil.reshape(pencil_flat), "space", split_axis=1, concat_axis=2, tiled=True
    )
    mixed = mixed_four.reshape(batch, slab, flat)
    grad_skip, grad_in, grad_out = mlp_grads
    grad_spec, grad_skip, grad_in, grad_out = lax.psum(
        (grad_spec, grad_skip, grad_in, grad_out), ("dp", "space")
    )
    return mixed, grad_fields, grad_spec, grad_skip, grad_in, grad_out


def dot(left, right):
    return jnp.dot(left, right, preferred_element_type=full)


def dot_rows(left, right):
    return lax.dot_general(left, right, (((0,), (0,)), ((), ())), preferred_element_type=full)


def stack(block):
    count = block.shape[1] // lanes
    return jnp.concatenate([block[:, lanes * j : lanes * (j + 1)] for j in range(count)], 0)


def store_rows(ref, rows):
    height = ref.shape[0]
    for j in range(ref.shape[1] // lanes):
        ref[:, lanes * j : lanes * (j + 1)] = rows[height * j : height * (j + 1)]


def unstack(rows, height):
    count = rows.shape[0] // height
    return jnp.concatenate([rows[height * j : height * (j + 1)] for j in range(count)], 1)


def gelu_pair(values):
    square = values * values
    gate = 0.5 + 0.5 * jnp.tanh(values * (gelu_scale + gelu_scale * gelu_cubic * square))
    result = values * gate
    slope = gate + result * (1.0 - gate) * (
        2.0 * gelu_scale + 6.0 * gelu_scale * gelu_cubic * square
    )
    return result, slope


def partial_kernel(table_ref, field_ref, other_ref, mine_ref):
    rows = dot(table_ref[0], field_ref[...]).astype(half)
    cut = other_ref.shape[0]
    other_ref[...] = rows[:cut]
    mine_ref[...] = rows[cut:]


def add_kernel(mine_ref, came_ref, *out_refs):
    height = out_refs[0].shape[0]
    total = mine_ref[...].astype(full) + came_ref[...].astype(full)
    for step, ref in enumerate(out_refs):
        ref[...] = total[height * (step + 1) : height * (step + 2)].astype(half)


def swap_halves(rows, height):
    place = lax.broadcasted_iota(jnp.int32, rows.shape, 0) % height
    middle = height // 2
    up = jnp.concatenate([rows[middle:], rows[:middle]], 0)
    down = jnp.concatenate([rows[-middle:], rows[:-middle]], 0)
    first = place < middle
    return jnp.where(first, up, down), jnp.where(first, -1.0, 1.0)


def by_mode(rows, height):
    middle = height // 2
    mode = lax.broadcasted_iota(jnp.int32, rows.shape, 0) % middle
    return jnp.concatenate(
        [jnp.where(mode == m, rows, 0.0).astype(half) for m in range(middle)], 1
    )


def gathered(refs):
    total = refs[0][...].astype(full)
    for ref in refs[1:]:
        total = total + ref[...].astype(full)
    return stack(total.astype(half).astype(full))


def modal_kernel(weight_ref, *refs):
    part_refs, (spectrum_ref, modal_ref) = refs[:-2], refs[-2:]
    height = modal_ref.shape[0]
    rows = gathered(part_refs)
    store_rows(spectrum_ref, rows.astype(half))
    both = dot(by_mode(rows, height), weight_ref[...])
    crossed, sign = swap_halves(both[:, lanes:], height)
    store_rows(modal_ref, (both[:, :lanes] + sign * crossed).astype(half))


def modal_back_kernel(weight_ref, spectrum_ref, before_ref, *refs):
    part_refs, (back_ref, grad_ref) = refs[:-2], refs[-2:]
    height = back_ref.shape[0]
    rows = gathered(part_refs)
    split = by_mode(rows, height)
    both = dot(split, weight_ref[...])
    crossed, sign = swap_halves(both[:, lanes:], height)
    store_rows(back_ref, (both[:, :lanes] - sign * crossed).astype(half))
    spectrum = stack(spectrum_ref[...].astype(full))
    turned, sign = swap_halves(spectrum, height)
    sums = dot_rows(split, jnp.concatenate([spectrum, sign * turned], 1).astype(half))
    width = lanes // 2
    for m in range(height // 2):
        top = sums[lanes * m : lanes * m + width]
        low = sums[lanes * m + width : lanes * (m + 1)]
        grad_ref[0, m] = before_ref[0, m] + top[:, :width] + low[:, width:lanes]
        grad_ref[1, m] = (
            before_ref[1, m] + top[:, lanes : lanes + width] + low[:, lanes + width :]
        )


def pointwise_kernel(
    tables_ref,
    field_ref,
    cotan_ref,
    mine_ref,
    came_ref,
    skip_ref,
    in_ref,
    out_ref,
    in_turned_ref,
    out_turned_ref,
    before_ref,
    mixed_in_ref,
    mixed_ref,
    grad_pre_ref,
    other_part_ref,
    mine_part_ref,
    grads_ref,
    sum_in,
    sum_out,
    sum_skip,
):
    del mixed_in_ref
    step = pl.program_id(0)

    @pl.when(step == 0)
    def _():
        sum_in[...] = jnp.zeros_like(sum_in)
        sum_out[...] = jnp.zeros_like(sum_out)
        sum_skip[...] = jnp.zeros_like(sum_skip)

    height = field_ref.shape[0]
    modal = jnp.concatenate([mine_ref[...], came_ref[...]], 0)
    spatial = dot(tables_ref[0], modal).astype(half).astype(full)
    fields = stack(field_ref[...])
    cotan = stack(cotan_ref[...])
    preact = stack(spatial) + dot(fields, skip_ref[...])
    activated, slope = gelu_pair(preact)
    activated = activated.astype(half)
    hidden, inner_slope = gelu_pair(dot(activated, in_ref[...]))
    hidden = hidden.astype(half)
    grad_inner = (dot(cotan, out_turned_ref[...]) * inner_slope).astype(half)
    store_rows(mixed_ref, dot(hidden, out_ref[...]).astype(half))
    grad_pre = (dot(grad_inner, in_turned_ref[...]) * slope).astype(half)
    sum_out[...] += dot_rows(cotan, hidden)
    sum_in[...] += dot_rows(activated, grad_inner)
    sum_skip[...] += dot_rows(grad_pre, fields)
    wide = unstack(grad_pre, height)
    grad_pre_ref[...] = wide
    rows = dot(tables_ref[1], wide).astype(half)
    cut = other_part_ref.shape[0]
    other_part_ref[...] = rows[:cut]
    mine_part_ref[...] = rows[cut:]

    @pl.when(step == pl.num_programs(0) - 1)
    def _():
        width = lanes // 2
        units = sum_in.shape[1] // 2
        grads_ref[:, :units] = (
            before_ref[:, :units] + sum_in[:width, :units] + sum_in[width:, units:]
        )
        grads_ref[:, units : 2 * units] = (
            before_ref[:, units : 2 * units] + sum_out[:width, :units] + sum_out[width:, units:]
        )
        grads_ref[:, 2 * units : 2 * units + width] = (
            before_ref[:, 2 * units : 2 * units + width]
            + sum_skip[:width, :width]
            + sum_skip[width:, width:]
        )


def final_kernel(table_ref, grad_pre_ref, mine_ref, came_ref, skip_ref, before_ref, out_ref):
    del before_ref
    height = out_ref.shape[0]
    spectrum = jnp.concatenate([mine_ref[...], came_ref[...]], 0)
    fields = dot(table_ref[0], spectrum)
    skipped = dot(stack(grad_pre_ref[...]), skip_ref[...])
    out_ref[...] = (fields + unstack(skipped, height)).astype(half)


def place_kernel(order_ref, *refs):
    block_refs, out_ref = refs[:-1], refs[-1]
    count = block_refs[0].shape[1]
    for i, ref in enumerate(block_refs):
        out_ref[:, pl.ds(order_ref[i] * count, count)] = ref[...]


def twice(matrix):
    blank = jnp.zeros_like(matrix)
    return jnp.concatenate(
        [jnp.concatenate([matrix, blank], -1), jnp.concatenate([blank, matrix], -1)], -2
    )


def fits(span, slab, flat, width, modes):
    return (
        span % 2 == 0
        and modes % span == 0
        and (2 * modes // span) % 8 == 0
        and slab % 16 == 0
        and 2 * width == lanes
        and flat % (chunks * 1024) == 0
    )


def slab_shards(features, cotangent, spec_weight, skip_weight, w_in, w_out):
    span = lax.axis_size("space")
    _, slab, flat = features.shape
    width, units = w_in.shape
    modes = spec_weight.shape[1]
    length = slab * span
    ring = span // 2
    owned = modes // span
    height = 2 * owned
    side = ring * height
    count = flat // chunks
    tile = 1024
    steps = count // tile

    forward_tab, inverse_tab = dft_tables(length, modes)

    def rows_of(device):
        first = np.arange(device * owned, (device + 1) * owned)
        return np.concatenate([first, modes + first])

    def device_tables(device):
        z, y = divmod(device, 2)
        here = slice(device * slab, (device + 1) * slab)
        send = np.concatenate(
            [rows_of((z + s) % ring * 2 + v) for v in (1 - y, y) for s in range(ring)]
        )
        take = np.concatenate(
            [rows_of((z - s) % ring * 2 + v) for v in (y, 1 - y) for s in range(ring)]
        )
        return (
            forward_tab[send][:, here],
            inverse_tab[here][:, take],
            inverse_tab[here][:, send].T,
            forward_tab[take][:, here].T,
        )

    me = lax.axis_index("space")
    every = [device_tables(d) for d in range(span)]
    send_fields, take_modal, send_grads, take_back = (
        jnp.asarray(np.stack([tables[i] for tables in every]))[me] for i in range(4)
    )

    def across(value):
        return lax.ppermute(value, "space", [(d, d ^ 1) for d in range(span)])

    def along(value, s):
        return lax.ppermute(value, "space", [(d, (d + 2 * s) % span) for d in range(span)])

    def call(kernel, grid, ins, outs, shapes, flops, **more):
        moved = sum(math.prod(s.shape) * s.dtype.itemsize for s in jax.tree.leaves(shapes))
        return pl.pallas_call(
            kernel,
            grid=grid,
            in_specs=ins,
            out_specs=outs,
            out_shape=shapes,
            cost_estimate=pl.CostEstimate(
                flops=flops, bytes_accessed=2 * moved, transcendentals=0
            ),
            compiler_params=pltpu.CompilerParams(vmem_limit_bytes=56 << 20),
            **more,
        )

    def whole(shape):
        return pl.BlockSpec(shape, lambda *_: (0,) * len(shape))

    def table_spec(number, shape):
        return pl.BlockSpec((number,) + shape, lambda *_: (0, 0, 0))

    def shape_of(*dims, kind=half):
        return jax.ShapeDtypeStruct(dims, kind)

    fields = features.reshape(slab, flat)
    cotan = cotangent.reshape(slab, flat)

    own_weight = lax.dynamic_slice_in_dim(spec_weight, me * owned, owned, 1)
    turned = own_weight.swapaxes(2, 3)
    ahead = jnp.concatenate([twice(turned[0]), twice(turned[1])], -1).reshape(-1, 2 * lanes)
    astern = jnp.concatenate([twice(own_weight[0]), twice(own_weight[1])], -1).reshape(
        -1, 2 * lanes
    )
    skip_ahead, skip_back = twice(skip_weight.T), twice(skip_weight)
    in_ahead, in_back = twice(w_in), twice(w_in.T)
    out_ahead, out_back = twice(w_out), twice(w_out.T)

    def at(rows, c):
        return pl.BlockSpec((rows, tile), lambda i, c=c: (0, c * steps + i))

    def in_chunk(rows):
        return pl.BlockSpec((rows, tile), lambda i: (0, i))

    def partial_transform(c):
        return call(
            partial_kernel,
            (steps,),
            [whole((1,) + send_fields.shape), at(slab, c)],
            [in_chunk(side), in_chunk(side)],
            [shape_of(side, count)] * 2,
            2 * slab * 2 * side * count,
        )(send_fields[None], fields)

    def scatter(other, mine):
        came = across(other)
        outgoing = call(
            add_kernel,
            (2,),
            [pl.BlockSpec((side, count // 2), lambda i: (0, i))] * 2,
            [pl.BlockSpec((height, count // 2), lambda i: (0, i))] * (ring - 1),
            [shape_of(height, count)] * (ring - 1),
            side * count,
        )(mine, came)
        return [mine, came] + [along(outgoing[s - 1], s) for s in range(1, ring)]

    part_spec = pl.BlockSpec((height, count), lambda i: (0, 0))

    def modal_forward(parts):
        return call(
            modal_kernel,
            (1,),
            [whole(ahead.shape)] + [part_spec] * len(parts),
            [part_spec] * 2,
            [shape_of(height, count)] * 2,
            2 * height * count * width * 2,
        )(ahead, *parts)

    def modal_backward(spectrum, before, parts):
        return call(
            modal_back_kernel,
            (1,),
            [whole(astern.shape), part_spec, whole(before.shape)] + [part_spec] * len(parts),
            [part_spec, whole(before.shape)],
            [shape_of(height, count), shape_of(*before.shape, kind=full)],
            2 * height * count * width * 4,
        )(astern, spectrum, before, *parts)

    def gather(block):
        mine = jnp.concatenate([block] + [along(block, s) for s in range(1, ring)], 0)
        return mine, across(mine)

    def pointwise_chunk(c, mine, came, grads, mixed):
        aliased = {} if mixed is None else {11: 0}
        if mixed is None:
            mixed = jnp.zeros((16, lanes), half)
        tables = jnp.stack([take_modal, send_grads])
        return call(
            pointwise_kernel,
            (steps,),
            [
                whole(tables.shape),
                at(slab, c),
                at(slab, c),
                in_chunk(side),
                in_chunk(side),
                whole(skip_ahead.shape),
                whole(in_ahead.shape),
                whole(out_ahead.shape),
                whole(in_back.shape),
                whole(out_back.shape),
                whole(grads.shape),
                pl.BlockSpec(memory_space=pl.ANY),
            ],
            [at(slab, c), in_chunk(slab), in_chunk(side), in_chunk(side), whole(grads.shape)],
            [
                shape_of(slab, flat),
                shape_of(slab, count),
                shape_of(side, count),
                shape_of(side, count),
                shape_of(*grads.shape, kind=full),
            ],
            12 * slab * count * units,
            scratch_shapes=[
                pltpu.VMEM((lanes, 2 * units), full),
                pltpu.VMEM((lanes, 2 * units), full),
                pltpu.VMEM((lanes, lanes), full),
            ],
            input_output_aliases=aliased,
        )(
            tables,
            fields,
            cotan,
            mine,
            came,
            skip_ahead,
            in_ahead,
            out_ahead,
            in_back,
            out_back,
            grads,
            mixed,
        )

    def final_chunk(c, grad_pre, mine, came, before):
        aliased = {} if before is None else {5: 0}
        if before is None:
            before = jnp.zeros((16, lanes), half)
        return call(
            final_kernel,
            (steps,),
            [
                whole((1,) + take_back.shape),
                in_chunk(slab),
                in_chunk(side),
                in_chunk(side),
                whole(skip_back.shape),
                pl.BlockSpec(memory_space=pl.ANY),
            ],
            at(slab, c),
            shape_of(slab, flat),
            4 * slab * 2 * side * count,
            input_output_aliases=aliased,
        )(take_back[None], grad_pre, mine, came, skip_back, before)

    scattered = [scatter(*partial_transform(c)) for c in range(chunks)]
    spectra, modals = zip(*[modal_forward(parts) for parts in scattered])
    views = [gather(modal) for modal in modals]
    grads = jnp.zeros((width, 2 * units + lanes), full)
    mixed = None
    grad_pres, scattered = [], []
    for c in range(chunks):
        mixed, grad_pre, other, mine, grads = pointwise_chunk(c, *views[c], grads, mixed)
        grad_pres.append(grad_pre)
        scattered.append(scatter(other, mine))
    grad_spec = jnp.zeros((2, owned, width, width), full)
    views = []
    for c in range(chunks):
        back, grad_spec = modal_backward(spectra[c], grad_spec, scattered[c])
        views.append(gather(back))
    grad_fields = None
    for c in range(chunks):
        grad_fields = final_chunk(c, grad_pres[c], *views[c], grad_fields)

    copies = lax.axis_size("dp")

    def pair_sums(value, axis, size):
        bit = 1
        while bit < size:
            value = value + lax.ppermute(value, axis, [(d, d ^ bit) for d in range(size)])
            bit *= 2
        return value

    grads = pair_sums(pair_sums(grads, "dp", copies), "space", span)
    grad_spec = pair_sums(grad_spec, "dp", copies)
    blocks = [grad_spec] + [along(grad_spec, s) for s in range(1, ring)]
    blocks = blocks + [across(block) for block in blocks]
    z, y = me // 2, me % 2
    order = jnp.stack(
        [(z - s) % ring * 2 + v for v in (y, 1 - y) for s in range(ring)]
    ).astype(jnp.int32)
    grad_spec = pl.pallas_call(
        place_kernel,
        in_specs=[pl.BlockSpec(memory_space=pltpu.SMEM)]
        + [pl.BlockSpec(memory_space=pltpu.VMEM)] * span,
        out_specs=pl.BlockSpec(memory_space=pltpu.VMEM),
        out_shape=shape_of(2, modes, width, width, kind=full),
    )(order, *blocks)
    grad_in = grads[:, :units]
    grad_out = grads[:, units : 2 * units].T
    grad_skip = grads[:, 2 * units : 2 * units + width]
    return (
        mixed.reshape(features.shape),
        grad_fields.reshape(features.shape),
        grad_spec,
        grad_skip,
        grad_in,
        grad_out,
    )


def shards(features, cotangent, spec_weight, skip_weight, w_in, w_out):
    span = lax.axis_size("space")
    copies = lax.axis_size("dp")
    batch, slab, flat = features.shape
    pairs = copies & (copies - 1) == 0 and span & (span - 1) == 0
    if batch == 1 and pairs and fits(span, slab, flat, w_in.shape[0], spec_weight.shape[1]):
        return slab_shards(features, cotangent, spec_weight, skip_weight, w_in, w_out)
    return pencil_shards(features, cotangent, spec_weight, skip_weight, w_in, w_out)


def solution(mesh):
    return jax.shard_map(
        shards,
        mesh=mesh,
        in_specs=(P("dp", "space", None), P("dp", "space", None), P(), P(), P(), P()),
        out_specs=(P("dp", "space", None), P("dp", "space", None), P(), P(), P(), P()),
        check_vma=False,
    )
```

```python
import functools
import math

import jax
import jax.numpy as jnp
import ml_dtypes
import numpy as np
from jax import lax
from jax.experimental import pallas as pl
from jax.experimental.pallas import tpu as pltpu
from jax.sharding import PartitionSpec as P

gelu_scale = math.sqrt(2.0 / math.pi)
gelu_cubic = 0.044715
half = jnp.bfloat16
full = jnp.float32
chunks = 4
lanes = 128


def gelu_tanh(values):
    inner = jnp.tanh(gelu_scale * (values + gelu_cubic * values * values * values))
    return 0.5 * values * (1.0 + inner)


def gelu_slope(values):
    inner = jnp.tanh(gelu_scale * (values + gelu_cubic * values * values * values))
    return 0.5 * (1.0 + inner) + 0.5 * values * (1.0 - inner * inner) * gelu_scale * (
        1.0 + 3.0 * gelu_cubic * values * values
    )


def dft_tables(length, modes):
    places = np.arange(length)
    freqs = np.arange(modes)
    phase = (freqs[:, None] * places[None, :] % length).astype(np.float32) * np.float32(
        2.0 * math.pi / length
    )
    cosine = np.cos(phase).astype(np.float32)
    sine = np.sin(phase).astype(np.float32)
    forward_tab = np.concatenate([cosine, -sine], 0).astype(ml_dtypes.bfloat16)
    factor = np.where(freqs == 0, 1.0, 2.0).astype(np.float32)[:, None] / np.float32(length)
    inverse_tab = np.concatenate([factor * cosine, -factor * sine], 0).T.astype(ml_dtypes.bfloat16)
    return forward_tab, inverse_tab


def contract(form, left, right):
    return jnp.einsum(form, left, right, preferred_element_type=full)


def spectral_forward(fields, forward_tab, inverse_tab, spec_weight):
    modes = spec_weight.shape[1]
    spectrum = contract("kx,bxpc->bkpc", forward_tab, fields).astype(half)
    real_part = spectrum[:, :modes]
    imag_part = spectrum[:, modes:]
    weight_real = spec_weight[0]
    weight_imag = spec_weight[1]
    out_real = contract("bmpc,moc->bmpo", real_part, weight_real) - contract(
        "bmpc,moc->bmpo", imag_part, weight_imag
    )
    out_imag = contract("bmpc,moc->bmpo", imag_part, weight_real) + contract(
        "bmpc,moc->bmpo", real_part, weight_imag
    )
    modal = jnp.concatenate([out_real, out_imag], 1).astype(half)
    spatial = lax.optimization_barrier(contract("xk,bkpo->bxpo", inverse_tab, modal).astype(half))
    return spectrum, spatial


def pointwise(fields, spatial, cotan, skip_weight, w_in, w_out):
    preact = spatial.astype(full) + contract("bxpc,oc->bxpo", fields, skip_weight)
    activated = gelu_tanh(preact).astype(half)
    inner = contract("bxpc,cf->bxpf", activated, w_in)
    hidden = gelu_tanh(inner).astype(half)
    mixed = contract("bxpf,fc->bxpc", hidden, w_out).astype(half)
    grad_inner = (contract("bxpc,fc->bxpf", cotan, w_out) * gelu_slope(inner)).astype(half)
    grad_out = contract("bxpf,bxpc->fc", hidden, cotan)
    grad_in = contract("bxpc,bxpf->cf", activated, grad_inner)
    grad_pre = (contract("bxpf,cf->bxpc", grad_inner, w_in) * gelu_slope(preact)).astype(half)
    grad_skip = contract("bxpo,bxpc->oc", grad_pre, fields)
    return mixed, grad_pre, (grad_skip, grad_in, grad_out)


def spectral_backward(spectrum, grad_pre, forward_tab, inverse_tab, spec_weight, skip_weight):
    modes = spec_weight.shape[1]
    real_part = spectrum[:, :modes]
    imag_part = spectrum[:, modes:]
    weight_real = spec_weight[0]
    weight_imag = spec_weight[1]
    grad_modal = contract("xk,bxpo->bkpo", inverse_tab, grad_pre).astype(half)
    grad_real = grad_modal[:, :modes]
    grad_imag = grad_modal[:, modes:]
    spec_real = contract("bmpo,bmpc->moc", grad_real, real_part) + contract(
        "bmpo,bmpc->moc", grad_imag, imag_part
    )
    spec_imag = contract("bmpo,bmpc->moc", grad_imag, real_part) - contract(
        "bmpo,bmpc->moc", grad_real, imag_part
    )
    back_real = contract("moc,bmpo->bmpc", weight_real, grad_real) + contract(
        "moc,bmpo->bmpc", weight_imag, grad_imag
    )
    back_imag = contract("moc,bmpo->bmpc", weight_real, grad_imag) - contract(
        "moc,bmpo->bmpc", weight_imag, grad_real
    )
    grad_spectrum = jnp.concatenate([back_real, back_imag], 1).astype(half)
    grad_fields = (
        contract("kx,bkpc->bxpc", forward_tab, grad_spectrum)
        + contract("bxpo,oc->bxpc", grad_pre, skip_weight)
    ).astype(half)
    return jnp.stack([spec_real, spec_imag], 0), grad_fields


def pencil_shards(features, cotangent, spec_weight, skip_weight, w_in, w_out):
    span = lax.axis_size("space")
    batch, slab, flat = features.shape
    width = skip_weight.shape[0]
    modes = spec_weight.shape[1]
    length = slab * span
    positions = flat // width
    columns = positions // span
    forward_tab, inverse_tab = (jnp.asarray(table) for table in dft_tables(length, modes))
    pencil_shape = (batch, length, columns, width)
    pencil_flat = (batch, length, columns * width)
    pencil_u = lax.all_to_all(features, "space", split_axis=2, concat_axis=1, tiled=True)
    spectrum, spatial = spectral_forward(
        pencil_u.reshape(pencil_shape), forward_tab, inverse_tab, spec_weight
    )
    spatial_slab = lax.all_to_all(
        spatial.reshape(pencil_flat), "space", split_axis=1, concat_axis=2, tiled=True
    )
    slab_shape = (batch, slab, positions, width)
    mixed_four, grad_pre, mlp_grads = pointwise(
        features.reshape(slab_shape),
        spatial_slab.reshape(slab_shape),
        cotangent.reshape(slab_shape),
        skip_weight,
        w_in,
        w_out,
    )
    pencil_grad = lax.all_to_all(
        grad_pre.reshape(batch, slab, flat), "space", split_axis=2, concat_axis=1, tiled=True
    )
    grad_spec, grad_pencil = spectral_backward(
        spectrum,
        pencil_grad.reshape(pencil_shape),
        forward_tab,
        inverse_tab,
        spec_weight,
        skip_weight,
    )
    grad_fields = lax.all_to_all(
        grad_pencil.reshape(pencil_flat), "space", split_axis=1, concat_axis=2, tiled=True
    )
    mixed = mixed_four.reshape(batch, slab, flat)
    grad_skip, grad_in, grad_out = mlp_grads
    grad_spec, grad_skip, grad_in, grad_out = lax.psum(
        (grad_spec, grad_skip, grad_in, grad_out), ("dp", "space")
    )
    return mixed, grad_fields, grad_spec, grad_skip, grad_in, grad_out


def dot(left, right):
    return jnp.dot(left, right, preferred_element_type=full)


def dot_rows(left, right):
    return lax.dot_general(left, right, (((0,), (0,)), ((), ())), preferred_element_type=full)


def stack(block):
    count = block.shape[1] // lanes
    return jnp.concatenate([block[:, lanes * j : lanes * (j + 1)] for j in range(count)], 0)


def store_rows(ref, rows):
    height = ref.shape[0]
    for j in range(ref.shape[1] // lanes):
        ref[:, lanes * j : lanes * (j + 1)] = rows[height * j : height * (j + 1)]


def unstack(rows, height):
    count = rows.shape[0] // height
    return jnp.concatenate([rows[height * j : height * (j + 1)] for j in range(count)], 1)


def gelu_pair(values):
    square = values * values
    gate = 0.5 + 0.5 * jnp.tanh(values * (gelu_scale + gelu_scale * gelu_cubic * square))
    result = values * gate
    slope = gate + result * (1.0 - gate) * (
        2.0 * gelu_scale + 6.0 * gelu_scale * gelu_cubic * square
    )
    return result, slope


def store_parts(refs, rows):
    rows = rows.astype(half)
    cut = refs[0].shape[0]
    for i, ref in enumerate(refs):
        ref[...] = rows[cut * i : cut * (i + 1)]


def join_parts(refs):
    return jnp.concatenate([ref[...] for ref in refs], 0)


def partial_kernel(table_ref, field_ref, *part_refs):
    store_parts(part_refs, dot(table_ref[0], field_ref[...]))


def swap_halves(rows, height):
    place = lax.broadcasted_iota(jnp.int32, rows.shape, 0) % height
    middle = height // 2
    up = jnp.concatenate([rows[middle:], rows[:middle]], 0)
    down = jnp.concatenate([rows[-middle:], rows[:-middle]], 0)
    first = place < middle
    return jnp.where(first, up, down), jnp.where(first, -1.0, 1.0)


def by_mode(rows, height):
    middle = height // 2
    mode = lax.broadcasted_iota(jnp.int32, rows.shape, 0) % middle
    return jnp.concatenate(
        [jnp.where(mode == m, rows, 0.0).astype(half) for m in range(middle)], 1
    )


def gathered(refs):
    total = refs[0][...].astype(full)
    for ref in refs[1:]:
        total = total + ref[...].astype(full)
    return stack(total.astype(half).astype(full))


def modal_kernel(weight_ref, *refs):
    part_refs, (spectrum_ref, modal_ref) = refs[:-2], refs[-2:]
    height = modal_ref.shape[0]
    rows = gathered(part_refs)
    store_rows(spectrum_ref, rows.astype(half))
    both = dot(by_mode(rows, height), weight_ref[...])
    crossed, sign = swap_halves(both[:, lanes:], height)
    store_rows(modal_ref, (both[:, :lanes] + sign * crossed).astype(half))


def modal_back_kernel(weight_ref, spectrum_ref, before_ref, *refs):
    part_refs, (back_ref, grad_ref) = refs[:-2], refs[-2:]
    height = back_ref.shape[0]
    rows = gathered(part_refs)
    split = by_mode(rows, height)
    both = dot(split, weight_ref[...])
    crossed, sign = swap_halves(both[:, lanes:], height)
    store_rows(back_ref, (both[:, :lanes] - sign * crossed).astype(half))
    spectrum = stack(spectrum_ref[...].astype(full))
    turned, sign = swap_halves(spectrum, height)
    sums = dot_rows(split, jnp.concatenate([spectrum, sign * turned], 1).astype(half))
    width = lanes // 2
    for m in range(height // 2):
        top = sums[lanes * m : lanes * m + width]
        low = sums[lanes * m + width : lanes * (m + 1)]
        grad_ref[0, m] = before_ref[0, m] + top[:, :width] + low[:, width:lanes]
        grad_ref[1, m] = (
            before_ref[1, m] + top[:, lanes : lanes + width] + low[:, lanes + width :]
        )


def pointwise_kernel(rings, aliased, *refs):
    tables_ref, field_ref, cotan_ref = refs[:3]
    modal_refs = refs[3 : 3 + rings]
    skip_ref, in_ref, out_ref, in_turned_ref, out_turned_ref, before_ref = refs[
        3 + rings : 9 + rings
    ]
    results = refs[9 + rings + aliased :]
    mixed_ref, grad_pre_ref, grads_ref = results[:3]
    part_refs = results[3 : 3 + rings]
    sum_in, sum_out, sum_skip = results[3 + rings :]
    step = pl.program_id(0)

    @pl.when(step == 0)
    def _():
        sum_in[...] = jnp.zeros_like(sum_in)
        sum_out[...] = jnp.zeros_like(sum_out)
        sum_skip[...] = jnp.zeros_like(sum_skip)

    height = field_ref.shape[0]
    spatial = dot(tables_ref[0], join_parts(modal_refs)).astype(half).astype(full)
    fields = stack(field_ref[...])
    cotan = stack(cotan_ref[...])
    preact = stack(spatial) + dot(fields, skip_ref[...])
    activated, slope = gelu_pair(preact)
    activated = activated.astype(half)
    hidden, inner_slope = gelu_pair(dot(activated, in_ref[...]))
    hidden = hidden.astype(half)
    grad_inner = (dot(cotan, out_turned_ref[...]) * inner_slope).astype(half)
    store_rows(mixed_ref, dot(hidden, out_ref[...]).astype(half))
    grad_pre = (dot(grad_inner, in_turned_ref[...]) * slope).astype(half)
    sum_out[...] += dot_rows(cotan, hidden)
    sum_in[...] += dot_rows(activated, grad_inner)
    sum_skip[...] += dot_rows(grad_pre, fields)
    wide = unstack(grad_pre, height)
    grad_pre_ref[...] = wide
    store_parts(part_refs, dot(tables_ref[1], wide))

    @pl.when(step == pl.num_programs(0) - 1)
    def _():
        width = lanes // 2
        units = sum_in.shape[1] // 2
        grads_ref[:, :units] = (
            before_ref[:, :units] + sum_in[:width, :units] + sum_in[width:, units:]
        )
        grads_ref[:, units : 2 * units] = (
            before_ref[:, units : 2 * units] + sum_out[:width, :units] + sum_out[width:, units:]
        )
        grads_ref[:, 2 * units : 2 * units + width] = (
            before_ref[:, 2 * units : 2 * units + width]
            + sum_skip[:width, :width]
            + sum_skip[width:, width:]
        )


def final_kernel(table_ref, grad_pre_ref, skip_ref, before_ref, *refs):
    del before_ref
    part_refs, out_ref = refs[:-1], refs[-1]
    height = out_ref.shape[0]
    fields = dot(table_ref[0], join_parts(part_refs))
    skipped = dot(stack(grad_pre_ref[...]), skip_ref[...])
    out_ref[...] = (fields + unstack(skipped, height)).astype(half)


def place_kernel(order_ref, *refs):
    block_refs, out_ref = refs[:-1], refs[-1]
    number = 0
    for ref in block_refs:
        for i in range(ref.shape[0]):
            count = ref.shape[2]
            out_ref[:, pl.ds(order_ref[number] * count, count)] = ref[i]
            number += 1


def twice(matrix):
    blank = jnp.zeros_like(matrix)
    return jnp.concatenate(
        [jnp.concatenate([matrix, blank], -1), jnp.concatenate([blank, matrix], -1)], -2
    )


def fits(span, slab, flat, width, modes):
    return (
        span == 8
        and modes % (2 * span) == 0
        and (2 * modes // span) % 8 == 0
        and slab % 16 == 0
        and 2 * width == lanes
        and flat % (chunks * 4096) == 0
    )


plan = (
    "K0 K1 K2 K3 A0 A1 A2 A3 B0 B1 B2 B3 C0 C1 M0 M1 C2 C3 D0 D1 M2 M3 E0 E1 D2 D3 F0 F1 "
    "P0 E2 p0 E3 P1 F2 p1 F3 a0 P2 a1 b0 p2 b1 c0 P3 c1 n0 p3 n1 S a2 d0 a3 d1 b2 b3 S e0 e1 "
    "c2 c3 S f0 f1 n2 n3 T S d2 d3 T S e2 e3 T Q0 f2 f3 T Q1 T T Q2 T Q3"
)


def slab_shards(features, cotangent, spec_weight, skip_weight, w_in, w_out):
    span = lax.axis_size("space")
    copies = lax.axis_size("dp")
    _, slab, flat = features.shape
    width, units = w_in.shape
    modes = spec_weight.shape[1]
    length = slab * span
    owned = modes // span
    height = 2 * owned
    rings = span // 2
    count = flat // chunks
    tile = 1024
    broad = min(4096, count)
    me = lax.axis_index("space")

    circle = [2 * z for z in range(rings)] + [2 * z + 1 for z in reversed(range(rings))]
    seat = {device: r for r, device in enumerate(circle)}

    def mate(device, pairing):
        r = seat[device]
        return circle[(r + (1 if r % 2 == pairing else -1)) % span]

    def swap(value, pairing):
        return lax.ppermute(value, "space", [(d, mate(d, pairing)) for d in range(span)])

    def holdings(first):
        blocks = {d: [d, mate(d, first)] for d in range(span)}
        last = blocks
        for step in range(1, rings):
            last = {d: last[mate(d, (first + step) % 2)] for d in range(span)}
            blocks = {d: blocks[d] + last[d] for d in range(span)}
        return blocks

    forward_tab, inverse_tab = dft_tables(length, modes)

    def rows_of(device):
        own = np.arange(device * owned, (device + 1) * owned)
        return np.concatenate([own, modes + own])

    def device_tables(device, order):
        here = slice(device * slab, (device + 1) * slab)
        rows = np.concatenate([rows_of(d) for d in order])
        return np.stack(
            [
                forward_tab[rows][:, here],
                inverse_tab[here][:, rows],
                inverse_tab[here][:, rows].T,
                forward_tab[rows][:, here].T,
            ]
        )

    tables = jnp.asarray(
        np.stack(
            [
                np.stack([device_tables(d, holdings(first)[d]) for first in range(2)])
                for d in range(span)
            ]
        )
    )[me]
    send_fields = [tables[first, :1] for first in range(2)]
    middle_tables = [tables[first, 1:3] for first in range(2)]
    take_back = [tables[first, 3:] for first in range(2)]

    def call(kernel, grid, ins, outs, shapes, **more):
        return pl.pallas_call(
            kernel,
            grid=grid,
            in_specs=ins,
            out_specs=outs,
            out_shape=shapes,
            cost_estimate=pl.CostEstimate(flops=1, bytes_accessed=1, transcendentals=0),
            compiler_params=pltpu.CompilerParams(vmem_limit_bytes=56 << 20),
            **more,
        )

    latest = []

    def after(value):
        if latest:
            value, _ = lax.optimization_barrier((value, latest[-1]))
        return value

    def done(results, mark=0):
        latest.append(results[mark])
        return results

    def pin(value):
        value = after(value)
        latest.append(value)
        return value

    def whole(shape):
        return pl.BlockSpec(shape, lambda *_: (0,) * len(shape))

    def shape_of(*dims, kind=half):
        return jax.ShapeDtypeStruct(dims, kind)

    fields = features.reshape(slab, flat)
    cotan = cotangent.reshape(slab, flat)

    own_weight = lax.dynamic_slice_in_dim(spec_weight, me * owned, owned, 1)
    turned = own_weight.swapaxes(2, 3)
    ahead = jnp.concatenate([twice(turned[0]), twice(turned[1])], -1).reshape(-1, 2 * lanes)
    astern = jnp.concatenate([twice(own_weight[0]), twice(own_weight[1])], -1).reshape(
        -1, 2 * lanes
    )
    skip_ahead, skip_back = twice(skip_weight.T), twice(skip_weight)
    in_ahead, in_back = twice(w_in), twice(w_in.T)
    out_ahead, out_back = twice(w_out), twice(w_out.T)

    def at(rows, c, size, first=0):
        return pl.BlockSpec((rows, size), lambda i: (0, c * (count // size) + first + i))

    def in_chunk(rows, size, first=0):
        return pl.BlockSpec((rows, size), lambda i: (0, first + i))

    pair = 2 * height
    part_spec = pl.BlockSpec((height, count), lambda i: (0, 0))

    def partial_transform(c):
        return done(
            call(
                partial_kernel,
                (count // broad,),
                [whole(send_fields[0].shape), at(slab, c, broad)],
                [in_chunk(pair, broad)] * rings,
                [shape_of(pair, count)] * rings,
            )(after(send_fields[c % 2]), fields)
        )

    def modal_forward(c, parts):
        return done(
            call(
                modal_kernel,
                (1,),
                [whole(ahead.shape)] + [part_spec] * len(parts),
                [part_spec] * 2,
                [shape_of(height, count)] * 2,
            )(after(ahead), *parts)
        )

    def modal_backward(spectrum, before, parts):
        return done(
            call(
                modal_back_kernel,
                (1,),
                [whole(astern.shape), part_spec, whole(before.shape)] + [part_spec] * len(parts),
                [part_spec, whole(before.shape)],
                [shape_of(height, count), shape_of(*before.shape, kind=full)],
            )(after(astern), spectrum, before, *parts)
        )

    def pointwise_part(c, number, modal, grads, buffers):
        steps = count // tile // 2
        first = number * steps
        shapes = [shape_of(slab, flat), shape_of(slab, count)]
        shapes += [shape_of(*grads.shape, kind=full)]
        shapes += [shape_of(pair, count)] * rings
        base = 9 + rings
        spots = [0] + [1] * (number > 0) + list(range(3, 3 + rings)) * (number > 0)
        given = [buffers[spot] for spot in spots if buffers[spot] is not None]
        spots = [spot for spot in spots if buffers[spot] is not None]
        return done(
            call(
                functools.partial(pointwise_kernel, rings, len(given)),
                (steps,),
                [
                    whole(middle_tables[0].shape),
                    at(slab, c, tile, first),
                    at(slab, c, tile, first),
                ]
                + [in_chunk(pair, tile, first)] * rings
                + [
                    whole(skip_ahead.shape),
                    whole(in_ahead.shape),
                    whole(out_ahead.shape),
                    whole(in_back.shape),
                    whole(out_back.shape),
                    whole(grads.shape),
                ]
                + [pl.BlockSpec(memory_space=pl.ANY)] * len(given),
                [
                    at(slab, c, tile, first),
                    in_chunk(slab, tile, first),
                    whole(grads.shape),
                ]
                + [in_chunk(pair, tile, first)] * rings,
                shapes,
                scratch_shapes=[
                    pltpu.VMEM((lanes, 2 * units), full),
                    pltpu.VMEM((lanes, 2 * units), full),
                    pltpu.VMEM((lanes, lanes), full),
                ],
                input_output_aliases={base + i: spot for i, spot in enumerate(spots)},
            )(
                after(middle_tables[c % 2]),
                fields,
                cotan,
                *modal,
                skip_ahead,
                in_ahead,
                out_ahead,
                in_back,
                out_back,
                grads,
                *given,
            ),
            2,
        )

    def final_chunk(c, grad_pre, parts, before):
        aliased = {} if before is None else {3: 0}
        if before is None:
            before = jnp.zeros((16, lanes), half)
        result = call(
            final_kernel,
            (count // broad,),
            [
                whole(take_back[0].shape),
                in_chunk(slab, broad),
                whole(skip_back.shape),
                pl.BlockSpec(memory_space=pl.ANY),
            ]
            + [in_chunk(pair, broad)] * rings,
            at(slab, c, broad),
            shape_of(slab, flat),
            input_output_aliases=aliased,
        )(after(take_back[c % 2]), grad_pre, skip_back, before, *parts)
        return result

    def add(left, right):
        return (left.astype(full) + right.astype(full)).astype(half)

    def beside(value, bit):
        return lax.ppermute(value, "dp", [(d, d ^ bit) for d in range(copies)])

    def summing(value):
        for i in range(copies.bit_length() - 1):
            value = after(value + beside(value, 1 << i))
            latest.append(value)
            yield value
        for i in range(span.bit_length() - 1):
            came = lax.ppermute(value, "space", [(d, d ^ (1 << i)) for d in range(span)])
            value = after(value + came)
            latest.append(value)
            yield value

    core = lax.axis_index("dp") % 2
    piece = owned // 2

    def collecting(value):
        kept = lax.dynamic_slice_in_dim(value, core * piece, piece, 1)
        given = lax.dynamic_slice_in_dim(value, (1 - core) * piece, piece, 1)
        kept = pin(kept + beside(given, 1))
        yield kept
        bit = 2
        while bit < copies:
            kept = pin(kept + beside(kept, bit))
            yield kept
            bit *= 2
        blocks = pin(jnp.stack([kept, swap(kept, 0)]))
        yield blocks
        held = [blocks]
        for step in range(1, rings):
            held.append(pin(swap(held[-1], step % 2)))
            yield held
        twins = [beside(value, 1) for value in held]
        order = jnp.asarray(np.array([holdings(0)[d] for d in range(span)], np.int32))[me]
        order = jnp.concatenate([order * 2 + core, order * 2 + 1 - core]).astype(jnp.int32)
        yield pl.pallas_call(
            place_kernel,
            in_specs=[pl.BlockSpec(memory_space=pltpu.SMEM)]
            + [pl.BlockSpec(memory_space=pltpu.VMEM)] * (2 * rings),
            out_specs=pl.BlockSpec(memory_space=pltpu.VMEM),
            out_shape=shape_of(2, modes, width, width, kind=full),
        )(order, *held, *twins)

    mixed = grad_fields = None
    grads = jnp.zeros((width, 2 * units + lanes), full)
    grad_spec = jnp.zeros((2, owned, width, width), full)
    parts, came, held, spectra, grad_pres = {}, {}, {}, {}, {}
    sums = pieces = None
    spec_result = None
    for job in plan.split():
        kind, c = job[0].upper(), int(job[1:] or 0)
        turn = c % 2

        def swapped(value, step, turn=turn):
            return swap(value, (turn + step) % 2)

        if kind == "K":
            parts[c] = partial_transform(c)
            came[c] = swapped(parts[c][-1], rings - 1)
        elif kind in "AB":
            step = rings - (2 if kind == "A" else 3)
            total = pin(add(parts[c][step], came[c]))
            came[c] = swapped(total, step)
        elif kind == "C":
            total = pin(add(parts[c][0][height:], came[c][height:]))
            parts[c] = [parts[c][0], came[c], swapped(total, 0)]
        elif job[0] == "M":
            spectra[c], modal = modal_forward(c, parts[c])
            held[c] = [modal, swapped(modal, 0)]
        elif job[0] == "n":
            back, grad_spec = modal_backward(spectra[c], grad_spec, parts[c])
            held[c] = [back, swapped(back, 0)]
        elif kind == "D":
            both = pin(jnp.concatenate(held[c], 0))
            held[c] = [both, swapped(both, 1)]
        elif kind in "EF":
            step = 2 if kind == "E" else 3
            last = pin(held[c][-1])
            held[c] = held[c][:-1] + [last, swapped(last, step)]
        elif kind == "P":
            number = int(job[0] == "p")
            buffers = [mixed, grad_pres.get(c), None] + list(parts[c] if number else [None] * rings)
            mixed, grad_pres[c], grads, *parts[c] = pointwise_part(
                c, number, held[c], grads, buffers
            )
            if number:
                came[c] = swapped(parts[c][-1], rings - 1)
        elif kind == "Q":
            grad_fields = final_chunk(c, grad_pres[c], held[c], grad_fields)
        elif kind == "S":
            sums = summing(grads) if sums is None else sums
            grads = next(sums)
        else:
            pieces = collecting(grad_spec) if pieces is None else pieces
            spec_result = next(pieces)
    for grads in sums:
        pass
    for spec_result in pieces:
        pass
    grad_spec = spec_result
    grad_in = grads[:, :units]
    grad_out = grads[:, units : 2 * units].T
    grad_skip = grads[:, 2 * units : 2 * units + width]
    return (
        mixed.reshape(features.shape),
        grad_fields.reshape(features.shape),
        grad_spec,
        grad_skip,
        grad_in,
        grad_out,
    )


def shards(features, cotangent, spec_weight, skip_weight, w_in, w_out):
    span = lax.axis_size("space")
    copies = lax.axis_size("dp")
    batch, slab, flat = features.shape
    pairs = copies % 2 == 0 and (copies * span) & (copies * span - 1) == 0
    if batch == 1 and pairs and fits(span, slab, flat, w_in.shape[0], spec_weight.shape[1]):
        return slab_shards(features, cotangent, spec_weight, skip_weight, w_in, w_out)
    return pencil_shards(features, cotangent, spec_weight, skip_weight, w_in, w_out)


def solution(mesh):
    return jax.shard_map(
        shards,
        mesh=mesh,
        in_specs=(P("dp", "space", None), P("dp", "space", None), P(), P(), P(), P()),
        out_specs=(P("dp", "space", None), P("dp", "space", None), P(), P(), P(), P()),
        check_vma=False,
    )
```

```python
import functools
import itertools
import math

import jax
import jax.numpy as jnp
import ml_dtypes
import numpy as np
from jax import lax
from jax.experimental import pallas as pl
from jax.experimental.pallas import tpu as pltpu
from jax.sharding import PartitionSpec as P

gelu_scale = math.sqrt(2.0 / math.pi)
gelu_cubic = 0.044715
half = jnp.bfloat16
full = jnp.float32
shares = (1, 1, 1, 1)
cuts = 1
lanes = 128


def gelu_tanh(values):
    inner = jnp.tanh(gelu_scale * (values + gelu_cubic * values * values * values))
    return 0.5 * values * (1.0 + inner)


def gelu_slope(values):
    inner = jnp.tanh(gelu_scale * (values + gelu_cubic * values * values * values))
    return 0.5 * (1.0 + inner) + 0.5 * values * (1.0 - inner * inner) * gelu_scale * (
        1.0 + 3.0 * gelu_cubic * values * values
    )


def dft_tables(length, modes):
    places = np.arange(length)
    freqs = np.arange(modes)
    phase = (freqs[:, None] * places[None, :] % length).astype(np.float32) * np.float32(
        2.0 * math.pi / length
    )
    cosine = np.cos(phase).astype(np.float32)
    sine = np.sin(phase).astype(np.float32)
    forward_tab = np.concatenate([cosine, -sine], 0).astype(ml_dtypes.bfloat16)
    factor = np.where(freqs == 0, 1.0, 2.0).astype(np.float32)[:, None] / np.float32(length)
    inverse_tab = np.concatenate([factor * cosine, -factor * sine], 0).T.astype(ml_dtypes.bfloat16)
    return forward_tab, inverse_tab


def contract(form, left, right):
    return jnp.einsum(form, left, right, preferred_element_type=full)


def spectral_forward(fields, forward_tab, inverse_tab, spec_weight):
    modes = spec_weight.shape[1]
    spectrum = contract("kx,bxpc->bkpc", forward_tab, fields).astype(half)
    real_part = spectrum[:, :modes]
    imag_part = spectrum[:, modes:]
    weight_real = spec_weight[0]
    weight_imag = spec_weight[1]
    out_real = contract("bmpc,moc->bmpo", real_part, weight_real) - contract(
        "bmpc,moc->bmpo", imag_part, weight_imag
    )
    out_imag = contract("bmpc,moc->bmpo", imag_part, weight_real) + contract(
        "bmpc,moc->bmpo", real_part, weight_imag
    )
    modal = jnp.concatenate([out_real, out_imag], 1).astype(half)
    spatial = lax.optimization_barrier(contract("xk,bkpo->bxpo", inverse_tab, modal).astype(half))
    return spectrum, spatial


def pointwise(fields, spatial, cotan, skip_weight, w_in, w_out):
    preact = spatial.astype(full) + contract("bxpc,oc->bxpo", fields, skip_weight)
    activated = gelu_tanh(preact).astype(half)
    inner = contract("bxpc,cf->bxpf", activated, w_in)
    hidden = gelu_tanh(inner).astype(half)
    mixed = contract("bxpf,fc->bxpc", hidden, w_out).astype(half)
    grad_inner = (contract("bxpc,fc->bxpf", cotan, w_out) * gelu_slope(inner)).astype(half)
    grad_out = contract("bxpf,bxpc->fc", hidden, cotan)
    grad_in = contract("bxpc,bxpf->cf", activated, grad_inner)
    grad_pre = (contract("bxpf,cf->bxpc", grad_inner, w_in) * gelu_slope(preact)).astype(half)
    grad_skip = contract("bxpo,bxpc->oc", grad_pre, fields)
    return mixed, grad_pre, (grad_skip, grad_in, grad_out)


def spectral_backward(spectrum, grad_pre, forward_tab, inverse_tab, spec_weight, skip_weight):
    modes = spec_weight.shape[1]
    real_part = spectrum[:, :modes]
    imag_part = spectrum[:, modes:]
    weight_real = spec_weight[0]
    weight_imag = spec_weight[1]
    grad_modal = contract("xk,bxpo->bkpo", inverse_tab, grad_pre).astype(half)
    grad_real = grad_modal[:, :modes]
    grad_imag = grad_modal[:, modes:]
    spec_real = contract("bmpo,bmpc->moc", grad_real, real_part) + contract(
        "bmpo,bmpc->moc", grad_imag, imag_part
    )
    spec_imag = contract("bmpo,bmpc->moc", grad_imag, real_part) - contract(
        "bmpo,bmpc->moc", grad_real, imag_part
    )
    back_real = contract("moc,bmpo->bmpc", weight_real, grad_real) + contract(
        "moc,bmpo->bmpc", weight_imag, grad_imag
    )
    back_imag = contract("moc,bmpo->bmpc", weight_real, grad_imag) - contract(
        "moc,bmpo->bmpc", weight_imag, grad_real
    )
    grad_spectrum = jnp.concatenate([back_real, back_imag], 1).astype(half)
    grad_fields = (
        contract("kx,bkpc->bxpc", forward_tab, grad_spectrum)
        + contract("bxpo,oc->bxpc", grad_pre, skip_weight)
    ).astype(half)
    return jnp.stack([spec_real, spec_imag], 0), grad_fields


def pencil_shards(features, cotangent, spec_weight, skip_weight, w_in, w_out):
    span = lax.axis_size("space")
    batch, slab, flat = features.shape
    width = skip_weight.shape[0]
    modes = spec_weight.shape[1]
    length = slab * span
    positions = flat // width
    columns = positions // span
    forward_tab, inverse_tab = (jnp.asarray(table) for table in dft_tables(length, modes))
    pencil_shape = (batch, length, columns, width)
    pencil_flat = (batch, length, columns * width)
    pencil_u = lax.all_to_all(features, "space", split_axis=2, concat_axis=1, tiled=True)
    spectrum, spatial = spectral_forward(
        pencil_u.reshape(pencil_shape), forward_tab, inverse_tab, spec_weight
    )
    spatial_slab = lax.all_to_all(
        spatial.reshape(pencil_flat), "space", split_axis=1, concat_axis=2, tiled=True
    )
    slab_shape = (batch, slab, positions, width)
    mixed_four, grad_pre, mlp_grads = pointwise(
        features.reshape(slab_shape),
        spatial_slab.reshape(slab_shape),
        cotangent.reshape(slab_shape),
        skip_weight,
        w_in,
        w_out,
    )
    pencil_grad = lax.all_to_all(
        grad_pre.reshape(batch, slab, flat), "space", split_axis=2, concat_axis=1, tiled=True
    )
    grad_spec, grad_pencil = spectral_backward(
        spectrum,
        pencil_grad.reshape(pencil_shape),
        forward_tab,
        inverse_tab,
        spec_weight,
        skip_weight,
    )
    grad_fields = lax.all_to_all(
        grad_pencil.reshape(pencil_flat), "space", split_axis=1, concat_axis=2, tiled=True
    )
    mixed = mixed_four.reshape(batch, slab, flat)
    grad_skip, grad_in, grad_out = mlp_grads
    grad_spec, grad_skip, grad_in, grad_out = lax.psum(
        (grad_spec, grad_skip, grad_in, grad_out), ("dp", "space")
    )
    return mixed, grad_fields, grad_spec, grad_skip, grad_in, grad_out


def dot(left, right):
    return jnp.dot(left, right, preferred_element_type=full)


def dot_rows(left, right):
    return lax.dot_general(left, right, (((0,), (0,)), ((), ())), preferred_element_type=full)


def stack(block):
    count = block.shape[1] // lanes
    return jnp.concatenate([block[:, lanes * j : lanes * (j + 1)] for j in range(count)], 0)


def store_rows(ref, rows):
    height = ref.shape[0]
    for j in range(ref.shape[1] // lanes):
        ref[:, lanes * j : lanes * (j + 1)] = rows[height * j : height * (j + 1)]


def unstack(rows, height):
    count = rows.shape[0] // height
    return jnp.concatenate([rows[height * j : height * (j + 1)] for j in range(count)], 1)


def gelu_pair(values):
    square = values * values
    gate = 0.5 + 0.5 * jnp.tanh(values * (gelu_scale + gelu_scale * gelu_cubic * square))
    result = values * gate
    slope = gate + result * (1.0 - gate) * (
        2.0 * gelu_scale + 6.0 * gelu_scale * gelu_cubic * square
    )
    return result, slope


def store_parts(refs, rows):
    rows = rows.astype(half)
    cut = refs[0].shape[0]
    for i, ref in enumerate(refs):
        ref[...] = rows[cut * i : cut * (i + 1)]


def join_parts(refs):
    return jnp.concatenate([ref[...] for ref in refs], 0)


def partial_kernel(table_ref, field_ref, *part_refs):
    store_parts(part_refs, dot(table_ref[0], field_ref[...]))


def swap_halves(rows, height):
    place = lax.broadcasted_iota(jnp.int32, rows.shape, 0) % height
    middle = height // 2
    up = jnp.concatenate([rows[middle:], rows[:middle]], 0)
    down = jnp.concatenate([rows[-middle:], rows[:-middle]], 0)
    first = place < middle
    return jnp.where(first, up, down), jnp.where(first, -1.0, 1.0)


def by_mode(rows, height, groups):
    place = lax.broadcasted_iota(jnp.int32, rows.shape, 0) % (height * groups)
    middle = height // 2
    mode = place // height * middle + place % middle
    return jnp.concatenate(
        [jnp.where(mode == m, rows, 0.0).astype(half) for m in range(middle * groups)], 1
    )


def gathered(refs):
    total = refs[0][...].astype(full)
    for ref in refs[1:-1]:
        total = total + ref[...].astype(full)
    middle = total.shape[0] // 2
    last = refs[-1][...].astype(full)
    total = total + jnp.concatenate([last[middle:], last[:middle]], 0)
    return stack(total.astype(half).astype(full))


def modal_kernel(height, weight_ref, *refs):
    part_refs, (spectrum_ref, modal_ref) = refs[:-2], refs[-2:]
    rows = gathered(part_refs)
    store_rows(spectrum_ref, rows.astype(half))
    both = dot(by_mode(rows, height, modal_ref.shape[0] // height), weight_ref[...])
    crossed, sign = swap_halves(both[:, lanes:], height)
    store_rows(modal_ref, (both[:, :lanes] + sign * crossed).astype(half))


def modal_back_kernel(height, weight_ref, spectrum_ref, before_ref, *refs):
    part_refs, (back_ref, grad_ref) = refs[:-2], refs[-2:]
    rows = gathered(part_refs)
    split = by_mode(rows, height, back_ref.shape[0] // height)
    both = dot(split, weight_ref[...])
    crossed, sign = swap_halves(both[:, lanes:], height)
    store_rows(back_ref, (both[:, :lanes] - sign * crossed).astype(half))
    spectrum = stack(spectrum_ref[...].astype(full))
    turned, sign = swap_halves(spectrum, height)
    own = height // 2
    sums = dot_rows(
        split[:, : lanes * own], jnp.concatenate([spectrum, sign * turned], 1).astype(half)
    )
    width = lanes // 2
    for m in range(own):
        top = sums[lanes * m : lanes * m + width]
        low = sums[lanes * m + width : lanes * (m + 1)]
        grad_ref[0, m] = before_ref[0, m] + top[:, :width] + low[:, width:lanes]
        grad_ref[1, m] = (
            before_ref[1, m] + top[:, lanes : lanes + width] + low[:, lanes + width :]
        )


def pointwise_kernel(rings, aliased, *refs):
    tables_ref, field_ref, cotan_ref = refs[:3]
    modal_refs = refs[3 : 3 + rings]
    skip_ref, in_ref, out_ref, in_turned_ref, out_turned_ref, before_ref = refs[
        3 + rings : 9 + rings
    ]
    results = refs[9 + rings + aliased :]
    mixed_ref, grad_pre_ref, grads_ref = results[:3]
    part_refs = results[3 : 3 + rings]
    sum_in, sum_out, sum_skip = results[3 + rings :]
    step = pl.program_id(0)

    @pl.when(step == 0)
    def _():
        sum_in[...] = jnp.zeros_like(sum_in)
        sum_out[...] = jnp.zeros_like(sum_out)
        sum_skip[...] = jnp.zeros_like(sum_skip)

    height = field_ref.shape[0]
    spatial = dot(tables_ref[0], join_parts(modal_refs)).astype(half).astype(full)
    fields = stack(field_ref[...])
    cotan = stack(cotan_ref[...])
    preact = stack(spatial) + dot(fields, skip_ref[...])
    activated, slope = gelu_pair(preact)
    activated = activated.astype(half)
    hidden, inner_slope = gelu_pair(dot(activated, in_ref[...]))
    hidden = hidden.astype(half)
    grad_inner = (dot(cotan, out_turned_ref[...]) * inner_slope).astype(half)
    store_rows(mixed_ref, dot(hidden, out_ref[...]).astype(half))
    grad_pre = (dot(grad_inner, in_turned_ref[...]) * slope).astype(half)
    sum_out[...] += dot_rows(cotan, hidden)
    sum_in[...] += dot_rows(activated, grad_inner)
    sum_skip[...] += dot_rows(grad_pre, fields)
    wide = unstack(grad_pre, height)
    grad_pre_ref[...] = wide
    store_parts(part_refs, dot(tables_ref[1], wide))

    @pl.when(step == pl.num_programs(0) - 1)
    def _():
        width = lanes // 2
        units = sum_in.shape[1] // 2
        grads_ref[:, :units] = (
            before_ref[:, :units] + sum_in[:width, :units] + sum_in[width:, units:]
        )
        grads_ref[:, units : 2 * units] = (
            before_ref[:, units : 2 * units] + sum_out[:width, :units] + sum_out[width:, units:]
        )
        grads_ref[:, 2 * units : 2 * units + width] = (
            before_ref[:, 2 * units : 2 * units + width]
            + sum_skip[:width, :width]
            + sum_skip[width:, width:]
        )


def final_kernel(table_ref, grad_pre_ref, skip_ref, before_ref, *refs):
    del before_ref
    part_refs, out_ref = refs[:-1], refs[-1]
    height = out_ref.shape[0]
    fields = dot(table_ref[0], join_parts(part_refs))
    skipped = dot(stack(grad_pre_ref[...]), skip_ref[...])
    out_ref[...] = (fields + unstack(skipped, height)).astype(half)


def place_kernel(order_ref, *refs):
    block_refs, out_ref = refs[:-1], refs[-1]
    number = 0
    for ref in block_refs:
        for i in range(ref.shape[0]):
            count = ref.shape[2]
            out_ref[:, pl.ds(order_ref[number] * count, count)] = ref[i]
            number += 1


def twice(matrix):
    blank = jnp.zeros_like(matrix)
    return jnp.concatenate(
        [jnp.concatenate([matrix, blank], -1), jnp.concatenate([blank, matrix], -1)], -2
    )


def fits(span, slab, flat, width, modes):
    return (
        span == 8
        and modes % (2 * span) == 0
        and (2 * modes // span) % 8 == 0
        and slab % 16 == 0
        and 2 * width == lanes
        and flat % (sum(shares) * 4096) == 0
    )


plan = (
    "K0 K1 K2 W",
    "A0 A1 K3 A2",
    "B0 B1 W A3",
    "C0 B2 W C1",
    "B3 M0 C2 M1",
    "C3 E0 M2 E1",
    "M3 F0 E2 F1",
    "E3 P0 F3 F2",
    "P1 P2 a0 a1",
    "P3 b0 a2 b1",
    "a3 c0 b2 b3",
    "S c1 c2 n0",
    "c3 n1 n2 e0",
    "n3 e1 e2 f0",
    "S e3 f1 f2",
    "T Q0 T S",
    "f3 T Q2 S",
    "T Q1 Q3 T",
    "S T T",
)


def slab_shards(features, cotangent, spec_weight, skip_weight, w_in, w_out):
    span = lax.axis_size("space")
    copies = lax.axis_size("dp")
    _, slab, flat = features.shape
    width, units = w_in.shape
    modes = spec_weight.shape[1]
    length = slab * span
    owned = modes // span
    height = 2 * owned
    rings = span // 2
    counts = [flat // sum(shares) * share for share in shares]
    starts = [sum(counts[:c]) for c in range(len(counts))]
    tile = 2048
    broad = 4096
    me = lax.axis_index("space")

    circle = [2 * z for z in range(rings)] + [2 * z + 1 for z in reversed(range(rings))]
    seat = {device: r for r, device in enumerate(circle)}

    def mate(device, pairing):
        r = seat[device]
        return circle[(r + (1 if r % 2 == pairing else -1)) % span]

    def swap(value, pairing):
        return lax.ppermute(value, "space", [(d, mate(d, pairing)) for d in range(span)])

    def holdings(first):
        blocks = {d: [d, mate(d, first)] for d in range(span)}
        last = blocks
        for step in range(1, rings):
            last = {d: last[mate(d, (first + step) % 2)] for d in range(span)}
            blocks = {d: blocks[d] + last[d] for d in range(span)}
        return blocks

    forward_tab, inverse_tab = dft_tables(length, modes)

    def rows_of(device):
        own = np.arange(device * owned, (device + 1) * owned)
        return np.concatenate([own, modes + own])

    def device_tables(device, order):
        here = slice(device * slab, (device + 1) * slab)
        rows = np.concatenate([rows_of(d) for d in order])
        return np.stack(
            [
                forward_tab[rows][:, here],
                inverse_tab[here][:, rows],
                inverse_tab[here][:, rows].T,
                forward_tab[rows][:, here].T,
            ]
        )

    tables = jnp.asarray(
        np.stack(
            [
                np.stack([device_tables(d, holdings(first)[d]) for first in range(2)])
                for d in range(span)
            ]
        )
    )[me]
    send_fields = [tables[first, :1] for first in range(2)]
    middle_tables = [tables[first, 1:3] for first in range(2)]
    take_back = [tables[first, 3:] for first in range(2)]

    token = jnp.zeros((8, lanes), full)

    def call(kernel, grid, ins, outs, shapes, scratch_shapes=(), aliases=()):
        near, far = len(ins), len(outs)

        def body(*refs):
            kernel(*refs[:near], *refs[near + 1 : near + 1 + far], *refs[near + 2 + far :])

        def run(*values):
            nonlocal token
            passed = pl.BlockSpec(memory_space=pl.ANY)
            *results, token = pl.pallas_call(
                body,
                grid=grid,
                in_specs=ins + [passed],
                out_specs=outs + [passed],
                out_shape=shapes + [jax.ShapeDtypeStruct(token.shape, token.dtype)],
                scratch_shapes=scratch_shapes,
                input_output_aliases=dict(aliases) | {near: far},
                cost_estimate=pl.CostEstimate(flops=1, bytes_accessed=1, transcendentals=0),
                compiler_params=pltpu.CompilerParams(vmem_limit_bytes=56 << 20),
            )(*values, token)
            return results

        return run

    def pin(value):
        nonlocal token
        value, token = lax.optimization_barrier((value, token))
        return value

    def whole(shape):
        return pl.BlockSpec(shape, lambda *_: (0,) * len(shape))

    def shape_of(*dims, kind=half):
        return jax.ShapeDtypeStruct(dims, kind)

    fields = features.reshape(slab, flat)
    cotan = cotangent.reshape(slab, flat)

    ahead, astern = [], []
    for first in range(2):
        other = jnp.asarray(np.array([mate(d, first) for d in range(span)], np.int32))[me]
        weight = jnp.concatenate(
            [lax.dynamic_slice_in_dim(spec_weight, d * owned, owned, 1) for d in (me, other)], 1
        )
        for result, matrix in ((ahead, weight.swapaxes(2, 3)), (astern, weight)):
            doubled = jnp.concatenate([twice(matrix[0]), twice(matrix[1])], -1)
            result.append(doubled.reshape(-1, 2 * lanes))
    skip_ahead, skip_back = twice(skip_weight.T), twice(skip_weight)
    in_ahead, in_back = twice(w_in), twice(w_in.T)
    out_ahead, out_back = twice(w_out), twice(w_out.T)

    def at(rows, c, size, first=0):
        return pl.BlockSpec((rows, size), lambda i: (0, starts[c] // size + first + i))

    def in_chunk(rows, size, first=0):
        return pl.BlockSpec((rows, size), lambda i: (0, first + i))

    pair = 2 * height
    def part_spec(c):
        return pl.BlockSpec((pair, counts[c]), lambda i: (0, 0))


    def partial_transform(c):
        return (
            call(
                partial_kernel,
                (counts[c] // broad,),
                [whole(send_fields[0].shape), at(slab, c, broad)],
                [in_chunk(pair, broad)] * rings,
                [shape_of(pair, counts[c])] * rings,
            )(send_fields[c % 2], fields)
        )

    def modal_forward(c, parts):
        return (
            call(
                functools.partial(modal_kernel, height),
                (1,),
                [whole(ahead[0].shape)] + [part_spec(c)] * len(parts),
                [part_spec(c)] * 2,
                [shape_of(pair, counts[c])] * 2,
            )(ahead[c % 2], *parts)
        )

    def modal_backward(c, spectrum, before, parts):
        return (
            call(
                functools.partial(modal_back_kernel, height),
                (1,),
                [whole(astern[0].shape), part_spec(c), whole(before.shape)] + [part_spec(c)] * len(parts),
                [part_spec(c), whole(before.shape)],
                [shape_of(pair, counts[c]), shape_of(*before.shape, kind=full)],
            )(astern[c % 2], spectrum, before, *parts)
        )

    def pointwise_part(c, number, modal, grads, buffers):
        steps = counts[c] // tile // cuts
        first = number * steps
        shapes = [shape_of(slab, flat), shape_of(slab, counts[c])]
        shapes += [shape_of(*grads.shape, kind=full)]
        shapes += [shape_of(pair, counts[c])] * rings
        base = 9 + rings
        spots = [0] + [1] * (number > 0) + list(range(3, 3 + rings)) * (number > 0)
        given = [buffers[spot] for spot in spots if buffers[spot] is not None]
        spots = [spot for spot in spots if buffers[spot] is not None]
        return (
            call(
                functools.partial(pointwise_kernel, rings, len(given)),
                (steps,),
                [
                    whole(middle_tables[0].shape),
                    at(slab, c, tile, first),
                    at(slab, c, tile, first),
                ]
                + [in_chunk(pair, tile, first)] * rings
                + [
                    whole(skip_ahead.shape),
                    whole(in_ahead.shape),
                    whole(out_ahead.shape),
                    whole(in_back.shape),
                    whole(out_back.shape),
                    whole(grads.shape),
                ]
                + [pl.BlockSpec(memory_space=pl.ANY)] * len(given),
                [
                    at(slab, c, tile, first),
                    in_chunk(slab, tile, first),
                    whole(grads.shape),
                ]
                + [in_chunk(pair, tile, first)] * rings,
                shapes,
                scratch_shapes=[
                    pltpu.VMEM((lanes, 2 * units), full),
                    pltpu.VMEM((lanes, 2 * units), full),
                    pltpu.VMEM((lanes, lanes), full),
                ],
                aliases={base + i: spot for i, spot in enumerate(spots)},
            )(
                middle_tables[c % 2],
                fields,
                cotan,
                *modal,
                skip_ahead,
                in_ahead,
                out_ahead,
                in_back,
                out_back,
                grads,
                *given,
            )
        )

    def final_chunk(c, grad_pre, parts, before):
        aliased = {} if before is None else {3: 0}
        if before is None:
            before = jnp.zeros((16, lanes), half)
        result = call(
            final_kernel,
            (counts[c] // broad,),
            [
                whole(take_back[0].shape),
                in_chunk(slab, broad),
                whole(skip_back.shape),
                pl.BlockSpec(memory_space=pl.ANY),
            ]
            + [in_chunk(pair, broad)] * rings,
            [at(slab, c, broad)],
            [shape_of(slab, flat)],
            aliases=aliased,
        )(take_back[c % 2], grad_pre, skip_back, before, *parts)
        return result[0]

    def add(left, right):
        return (left.astype(full) + right.astype(full)).astype(half)

    def beside(value, bit):
        return lax.ppermute(value, "dp", [(d, d ^ bit) for d in range(copies)])

    def summing(value):
        for i in range(copies.bit_length() - 1):
            value = pin(value + beside(value, 1 << i))
            yield value
        for i in range(span.bit_length() - 1):
            came = lax.ppermute(value, "space", [(d, d ^ (1 << i)) for d in range(span)])
            value = pin(value + came)
            yield value

    core = lax.axis_index("dp") % 2
    piece = owned // 2

    def collecting(value):
        kept = lax.dynamic_slice_in_dim(value, core * piece, piece, 1)
        given = lax.dynamic_slice_in_dim(value, (1 - core) * piece, piece, 1)
        kept = pin(kept + beside(given, 1))
        yield kept
        bit = 2
        while bit < copies:
            kept = pin(kept + beside(kept, bit))
            yield kept
            bit *= 2
        blocks = pin(jnp.stack([kept, swap(kept, 0)]))
        yield blocks
        held = [blocks]
        for step in range(1, rings):
            held.append(pin(swap(held[-1], step % 2)))
            yield held
        twins = [beside(value, 1) for value in held]
        order = jnp.asarray(np.array([holdings(0)[d] for d in range(span)], np.int32))[me]
        order = jnp.concatenate([order * 2 + core, order * 2 + 1 - core]).astype(jnp.int32)
        yield pl.pallas_call(
            place_kernel,
            in_specs=[pl.BlockSpec(memory_space=pltpu.SMEM)]
            + [pl.BlockSpec(memory_space=pltpu.VMEM)] * (2 * rings),
            out_specs=pl.BlockSpec(memory_space=pltpu.VMEM),
            out_shape=shape_of(2, modes, width, width, kind=full),
        )(order, *held, *twins)

    mixed = grad_fields = None
    grads = jnp.zeros((width, 2 * units + lanes), full)
    grad_spec = jnp.zeros((2, owned, width, width), full)
    parts, came, held, spectra, grad_pres = {}, {}, {}, {}, {}
    sums = pieces = None
    weights = 0
    spec_result = None
    for job in itertools.chain.from_iterable(jobs.split() for jobs in plan):
        kind, c = job[0].upper(), int(job[1:] or 0)
        turn = c % 2

        def swapped(value, step, turn=turn):
            return swap(value, (turn + step) % 2)

        if kind == "W":
            if weights == 0:
                ahead = pin(ahead)
            elif weights == 1:
                skip_ahead, in_ahead, in_back, out_ahead, out_back = pin(
                    (skip_ahead, in_ahead, in_back, out_ahead, out_back)
                )
            else:
                astern, skip_back = pin((astern, skip_back))
            weights += 1
        elif kind == "K":
            parts[c] = partial_transform(c)
            came[c] = swapped(parts[c][-1], rings - 1)
        elif kind in "AB":
            step = rings - (2 if kind == "A" else 3)
            total = pin(add(parts[c][step], came[c]))
            came[c] = swapped(total, step)
        elif kind == "C":
            total = pin(add(parts[c][0], came[c]))
            parts[c] = [parts[c][0], came[c], swapped(total, 0)]
        elif job[0] == "M":
            spectra[c], modal = modal_forward(c, parts[c])
            held[c] = [modal, swapped(modal, 1)]
        elif job[0] == "n":
            back, grad_spec = modal_backward(c, spectra[c], grad_spec, parts[c])
            held[c] = [back, swapped(back, 1)]
        elif kind in "EF":
            step = 2 if kind == "E" else 3
            last = pin(held[c][-1])
            held[c] = held[c][:-1] + [last, swapped(last, step)]
        elif kind == "P":
            number = int(job[0] == "p")
            buffers = [mixed, grad_pres.get(c), None] + list(parts[c] if number else [None] * rings)
            mixed, grad_pres[c], grads, *parts[c] = pointwise_part(
                c, number, held[c], grads, buffers
            )
            if number == cuts - 1:
                came[c] = swapped(parts[c][-1], rings - 1)
        elif kind == "Q":
            grad_fields = final_chunk(c, grad_pres[c], held[c], grad_fields)
        elif kind == "S":
            sums = summing(grads) if sums is None else sums
            grads = next(sums)
        else:
            pieces = collecting(grad_spec) if pieces is None else pieces
            spec_result = next(pieces)
    for grads in sums:
        pass
    for spec_result in pieces:
        pass
    grad_spec = spec_result
    grad_in = grads[:, :units]
    grad_out = grads[:, units : 2 * units].T
    grad_skip = grads[:, 2 * units : 2 * units + width]
    return (
        mixed.reshape(features.shape),
        grad_fields.reshape(features.shape),
        grad_spec,
        grad_skip,
        grad_in,
        grad_out,
    )


def shards(features, cotangent, spec_weight, skip_weight, w_in, w_out):
    span = lax.axis_size("space")
    copies = lax.axis_size("dp")
    batch, slab, flat = features.shape
    pairs = copies % 2 == 0 and (copies * span) & (copies * span - 1) == 0
    if batch == 1 and pairs and fits(span, slab, flat, w_in.shape[0], spec_weight.shape[1]):
        return slab_shards(features, cotangent, spec_weight, skip_weight, w_in, w_out)
    return pencil_shards(features, cotangent, spec_weight, skip_weight, w_in, w_out)


def solution(mesh):
    return jax.shard_map(
        shards,
        mesh=mesh,
        in_specs=(P("dp", "space", None), P("dp", "space", None), P(), P(), P(), P()),
        out_specs=(P("dp", "space", None), P("dp", "space", None), P(), P(), P(), P()),
        check_vma=False,
    )
```

```python
import functools
import itertools
import math

import jax
import jax.numpy as jnp
import ml_dtypes
import numpy as np
from jax import lax
from jax.experimental import pallas as pl
from jax.experimental.pallas import tpu as pltpu
from jax.sharding import PartitionSpec as P

gelu_scale = math.sqrt(2.0 / math.pi)
gelu_cubic = 0.044715
half = jnp.bfloat16
full = jnp.float32
shares = (1, 1, 1, 1)
cuts = 1
lanes = 128


def gelu_tanh(values):
    inner = jnp.tanh(gelu_scale * (values + gelu_cubic * values * values * values))
    return 0.5 * values * (1.0 + inner)


def gelu_slope(values):
    inner = jnp.tanh(gelu_scale * (values + gelu_cubic * values * values * values))
    return 0.5 * (1.0 + inner) + 0.5 * values * (1.0 - inner * inner) * gelu_scale * (
        1.0 + 3.0 * gelu_cubic * values * values
    )


def dft_tables(length, modes):
    places = np.arange(length)
    freqs = np.arange(modes)
    phase = (freqs[:, None] * places[None, :] % length).astype(np.float32) * np.float32(
        2.0 * math.pi / length
    )
    cosine = np.cos(phase).astype(np.float32)
    sine = np.sin(phase).astype(np.float32)
    forward_tab = np.concatenate([cosine, -sine], 0).astype(ml_dtypes.bfloat16)
    factor = np.where(freqs == 0, 1.0, 2.0).astype(np.float32)[:, None] / np.float32(length)
    inverse_tab = np.concatenate([factor * cosine, -factor * sine], 0).T.astype(ml_dtypes.bfloat16)
    return forward_tab, inverse_tab


def contract(form, left, right):
    return jnp.einsum(form, left, right, preferred_element_type=full)


def spectral_forward(fields, forward_tab, inverse_tab, spec_weight):
    modes = spec_weight.shape[1]
    spectrum = contract("kx,bxpc->bkpc", forward_tab, fields).astype(half)
    real_part = spectrum[:, :modes]
    imag_part = spectrum[:, modes:]
    weight_real = spec_weight[0]
    weight_imag = spec_weight[1]
    out_real = contract("bmpc,moc->bmpo", real_part, weight_real) - contract(
        "bmpc,moc->bmpo", imag_part, weight_imag
    )
    out_imag = contract("bmpc,moc->bmpo", imag_part, weight_real) + contract(
        "bmpc,moc->bmpo", real_part, weight_imag
    )
    modal = jnp.concatenate([out_real, out_imag], 1).astype(half)
    spatial = lax.optimization_barrier(contract("xk,bkpo->bxpo", inverse_tab, modal).astype(half))
    return spectrum, spatial


def pointwise(fields, spatial, cotan, skip_weight, w_in, w_out):
    preact = spatial.astype(full) + contract("bxpc,oc->bxpo", fields, skip_weight)
    activated = gelu_tanh(preact).astype(half)
    inner = contract("bxpc,cf->bxpf", activated, w_in)
    hidden = gelu_tanh(inner).astype(half)
    mixed = contract("bxpf,fc->bxpc", hidden, w_out).astype(half)
    grad_inner = (contract("bxpc,fc->bxpf", cotan, w_out) * gelu_slope(inner)).astype(half)
    grad_out = contract("bxpf,bxpc->fc", hidden, cotan)
    grad_in = contract("bxpc,bxpf->cf", activated, grad_inner)
    grad_pre = (contract("bxpf,cf->bxpc", grad_inner, w_in) * gelu_slope(preact)).astype(half)
    grad_skip = contract("bxpo,bxpc->oc", grad_pre, fields)
    return mixed, grad_pre, (grad_skip, grad_in, grad_out)


def spectral_backward(spectrum, grad_pre, forward_tab, inverse_tab, spec_weight, skip_weight):
    modes = spec_weight.shape[1]
    real_part = spectrum[:, :modes]
    imag_part = spectrum[:, modes:]
    weight_real = spec_weight[0]
    weight_imag = spec_weight[1]
    grad_modal = contract("xk,bxpo->bkpo", inverse_tab, grad_pre).astype(half)
    grad_real = grad_modal[:, :modes]
    grad_imag = grad_modal[:, modes:]
    spec_real = contract("bmpo,bmpc->moc", grad_real, real_part) + contract(
        "bmpo,bmpc->moc", grad_imag, imag_part
    )
    spec_imag = contract("bmpo,bmpc->moc", grad_imag, real_part) - contract(
        "bmpo,bmpc->moc", grad_real, imag_part
    )
    back_real = contract("moc,bmpo->bmpc", weight_real, grad_real) + contract(
        "moc,bmpo->bmpc", weight_imag, grad_imag
    )
    back_imag = contract("moc,bmpo->bmpc", weight_real, grad_imag) - contract(
        "moc,bmpo->bmpc", weight_imag, grad_real
    )
    grad_spectrum = jnp.concatenate([back_real, back_imag], 1).astype(half)
    grad_fields = (
        contract("kx,bkpc->bxpc", forward_tab, grad_spectrum)
        + contract("bxpo,oc->bxpc", grad_pre, skip_weight)
    ).astype(half)
    return jnp.stack([spec_real, spec_imag], 0), grad_fields


def pencil_shards(features, cotangent, spec_weight, skip_weight, w_in, w_out):
    span = lax.axis_size("space")
    batch, slab, flat = features.shape
    width = skip_weight.shape[0]
    modes = spec_weight.shape[1]
    length = slab * span
    positions = flat // width
    columns = positions // span
    forward_tab, inverse_tab = (jnp.asarray(table) for table in dft_tables(length, modes))
    pencil_shape = (batch, length, columns, width)
    pencil_flat = (batch, length, columns * width)
    pencil_u = lax.all_to_all(features, "space", split_axis=2, concat_axis=1, tiled=True)
    spectrum, spatial = spectral_forward(
        pencil_u.reshape(pencil_shape), forward_tab, inverse_tab, spec_weight
    )
    spatial_slab = lax.all_to_all(
        spatial.reshape(pencil_flat), "space", split_axis=1, concat_axis=2, tiled=True
    )
    slab_shape = (batch, slab, positions, width)
    mixed_four, grad_pre, mlp_grads = pointwise(
        features.reshape(slab_shape),
        spatial_slab.reshape(slab_shape),
        cotangent.reshape(slab_shape),
        skip_weight,
        w_in,
        w_out,
    )
    pencil_grad = lax.all_to_all(
        grad_pre.reshape(batch, slab, flat), "space", split_axis=2, concat_axis=1, tiled=True
    )
    grad_spec, grad_pencil = spectral_backward(
        spectrum,
        pencil_grad.reshape(pencil_shape),
        forward_tab,
        inverse_tab,
        spec_weight,
        skip_weight,
    )
    grad_fields = lax.all_to_all(
        grad_pencil.reshape(pencil_flat), "space", split_axis=1, concat_axis=2, tiled=True
    )
    mixed = mixed_four.reshape(batch, slab, flat)
    grad_skip, grad_in, grad_out = mlp_grads
    grad_spec, grad_skip, grad_in, grad_out = lax.psum(
        (grad_spec, grad_skip, grad_in, grad_out), ("dp", "space")
    )
    return mixed, grad_fields, grad_spec, grad_skip, grad_in, grad_out


def dot(left, right):
    return jnp.dot(left, right, preferred_element_type=full)


def dot_rows(left, right):
    return lax.dot_general(left, right, (((0,), (0,)), ((), ())), preferred_element_type=full)


def stack(block):
    count = block.shape[1] // lanes
    return jnp.concatenate([block[:, lanes * j : lanes * (j + 1)] for j in range(count)], 0)


def store_rows(ref, rows):
    height = ref.shape[0]
    for j in range(ref.shape[1] // lanes):
        ref[:, lanes * j : lanes * (j + 1)] = rows[height * j : height * (j + 1)]


def unstack(rows, height):
    count = rows.shape[0] // height
    return jnp.concatenate([rows[height * j : height * (j + 1)] for j in range(count)], 1)


def gelu_pair(values):
    square = values * values
    gate = 0.5 + 0.5 * jnp.tanh(values * (gelu_scale + gelu_scale * gelu_cubic * square))
    result = values * gate
    slope = gate + result * (1.0 - gate) * (
        2.0 * gelu_scale + 6.0 * gelu_scale * gelu_cubic * square
    )
    return result, slope


def store_parts(refs, rows):
    rows = rows.astype(half)
    cut = refs[0].shape[0]
    for i, ref in enumerate(refs):
        ref[...] = rows[cut * i : cut * (i + 1)]


def join_parts(refs):
    return jnp.concatenate([ref[...] for ref in refs], 0)


def partial_kernel(table_ref, field_ref, *part_refs):
    store_parts(part_refs, dot(table_ref[0], field_ref[...]))


def swap_halves(rows, height):
    place = lax.broadcasted_iota(jnp.int32, rows.shape, 0) % height
    middle = height // 2
    up = jnp.concatenate([rows[middle:], rows[:middle]], 0)
    down = jnp.concatenate([rows[-middle:], rows[:-middle]], 0)
    first = place < middle
    return jnp.where(first, up, down), jnp.where(first, -1.0, 1.0)


def by_mode(rows, height, groups):
    place = lax.broadcasted_iota(jnp.int32, rows.shape, 0) % (height * groups)
    middle = height // 2
    mode = place // height * middle + place % middle
    return jnp.concatenate(
        [jnp.where(mode == m, rows, 0.0).astype(half) for m in range(middle * groups)], 1
    )


def gathered(refs):
    total = refs[0][...].astype(full)
    for ref in refs[1:-1]:
        total = total + ref[...].astype(full)
    middle = total.shape[0] // 2
    last = refs[-1][...].astype(full)
    total = total + jnp.concatenate([last[middle:], last[:middle]], 0)
    return stack(total.astype(half).astype(full))


def modal_kernel(height, weight_ref, *refs):
    part_refs, (spectrum_ref, modal_ref) = refs[:-2], refs[-2:]
    rows = gathered(part_refs)
    store_rows(spectrum_ref, rows.astype(half))
    both = dot(by_mode(rows, height, modal_ref.shape[0] // height), weight_ref[...])
    crossed, sign = swap_halves(both[:, lanes:], height)
    store_rows(modal_ref, (both[:, :lanes] + sign * crossed).astype(half))


def modal_back_kernel(height, weight_ref, spectrum_ref, before_ref, *refs):
    part_refs, (back_ref, grad_ref) = refs[:-2], refs[-2:]
    rows = gathered(part_refs)
    split = by_mode(rows, height, back_ref.shape[0] // height)
    both = dot(split, weight_ref[...])
    crossed, sign = swap_halves(both[:, lanes:], height)
    store_rows(back_ref, (both[:, :lanes] - sign * crossed).astype(half))
    spectrum = stack(spectrum_ref[...].astype(full))
    turned, sign = swap_halves(spectrum, height)
    own = height // 2
    sums = dot_rows(
        split[:, : lanes * own], jnp.concatenate([spectrum, sign * turned], 1).astype(half)
    )
    width = lanes // 2
    for m in range(own):
        top = sums[lanes * m : lanes * m + width]
        low = sums[lanes * m + width : lanes * (m + 1)]
        grad_ref[0, m] = before_ref[0, m] + top[:, :width] + low[:, width:lanes]
        grad_ref[1, m] = (
            before_ref[1, m] + top[:, lanes : lanes + width] + low[:, lanes + width :]
        )


def pointwise_kernel(rings, aliased, *refs):
    tables_ref, field_ref, cotan_ref = refs[:3]
    modal_refs = refs[3 : 3 + rings]
    skip_ref, in_ref, out_ref, in_turned_ref, out_turned_ref, before_ref = refs[
        3 + rings : 9 + rings
    ]
    results = refs[9 + rings + aliased :]
    mixed_ref, grad_pre_ref, grads_ref = results[:3]
    part_refs = results[3 : 3 + rings]
    sum_in, sum_out, sum_skip = results[3 + rings :]
    step = pl.program_id(0)

    @pl.when(step == 0)
    def _():
        sum_in[...] = jnp.zeros_like(sum_in)
        sum_out[...] = jnp.zeros_like(sum_out)
        sum_skip[...] = jnp.zeros_like(sum_skip)

    height = field_ref.shape[0]
    spatial = dot(tables_ref[0], join_parts(modal_refs)).astype(half).astype(full)
    fields = stack(field_ref[...])
    cotan = stack(cotan_ref[...])
    preact = stack(spatial) + dot(fields, skip_ref[...])
    activated, slope = gelu_pair(preact)
    activated = activated.astype(half)
    hidden, inner_slope = gelu_pair(dot(activated, in_ref[...]))
    hidden = hidden.astype(half)
    grad_inner = (dot(cotan, out_turned_ref[...]) * inner_slope).astype(half)
    store_rows(mixed_ref, dot(hidden, out_ref[...]).astype(half))
    grad_pre = (dot(grad_inner, in_turned_ref[...]) * slope).astype(half)
    sum_out[...] += dot_rows(cotan, hidden)
    sum_in[...] += dot_rows(activated, grad_inner)
    sum_skip[...] += dot_rows(grad_pre, fields)
    wide = unstack(grad_pre, height)
    grad_pre_ref[...] = wide
    store_parts(part_refs, dot(tables_ref[1], wide))

    @pl.when(step == pl.num_programs(0) - 1)
    def _():
        width = lanes // 2
        units = sum_in.shape[1] // 2
        grads_ref[:, :units] = (
            before_ref[:, :units] + sum_in[:width, :units] + sum_in[width:, units:]
        )
        grads_ref[:, units : 2 * units] = (
            before_ref[:, units : 2 * units] + sum_out[:width, :units] + sum_out[width:, units:]
        )
        grads_ref[:, 2 * units : 2 * units + width] = (
            before_ref[:, 2 * units : 2 * units + width]
            + sum_skip[:width, :width]
            + sum_skip[width:, width:]
        )


def final_kernel(table_ref, grad_pre_ref, skip_ref, before_ref, *refs):
    del before_ref
    part_refs, out_ref = refs[:-1], refs[-1]
    height = out_ref.shape[0]
    fields = dot(table_ref[0], join_parts(part_refs))
    skipped = dot(stack(grad_pre_ref[...]), skip_ref[...])
    out_ref[...] = (fields + unstack(skipped, height)).astype(half)


def place_kernel(order_ref, *refs):
    block_refs, out_ref = refs[:-1], refs[-1]
    number = 0
    for ref in block_refs:
        for i in range(ref.shape[0]):
            count = ref.shape[2]
            out_ref[:, pl.ds(order_ref[number] * count, count)] = ref[i]
            number += 1


def twice(matrix):
    blank = jnp.zeros_like(matrix)
    return jnp.concatenate(
        [jnp.concatenate([matrix, blank], -1), jnp.concatenate([blank, matrix], -1)], -2
    )


def fits(span, slab, flat, width, modes):
    return (
        span == 8
        and modes % (2 * span) == 0
        and (2 * modes // span) % 8 == 0
        and slab % 16 == 0
        and 2 * width == lanes
        and flat % (sum(shares) * 4096) == 0
    )


plan = (
    "K0 K1 K2 W",
    "A0 A1 K3 A2",
    "B0 B1 W A3",
    "C0 B2 W C1",
    "B3 M0 C2 M1",
    "C3 E0 M2 E1",
    "M3 F0 E2 F1",
    "E3 P0 F3 F2",
    "P1 P2 a0 a1",
    "P3 b0 a2 b1",
    "a3 c0 b2 b3",
    "S c1 c2 n0",
    "c3 n1 n2 e0",
    "n3 e1 e2 f0",
    "T e3 f1 f2",
    "T Q0 f3 T",
    "S Q1 T S",
    "Q2 T S Q3",
    "T S T",
)


def slab_shards(features, cotangent, spec_weight, skip_weight, w_in, w_out):
    span = lax.axis_size("space")
    copies = lax.axis_size("dp")
    _, slab, flat = features.shape
    width, units = w_in.shape
    modes = spec_weight.shape[1]
    length = slab * span
    owned = modes // span
    height = 2 * owned
    rings = span // 2
    counts = [flat // sum(shares) * share for share in shares]
    starts = [sum(counts[:c]) for c in range(len(counts))]
    tile = 2048
    broad = 4096
    me = lax.axis_index("space")

    circle = [2 * z for z in range(rings)] + [2 * z + 1 for z in reversed(range(rings))]
    seat = {device: r for r, device in enumerate(circle)}

    def mate(device, pairing):
        r = seat[device]
        return circle[(r + (1 if r % 2 == pairing else -1)) % span]

    def swap(value, pairing):
        return lax.ppermute(value, "space", [(d, mate(d, pairing)) for d in range(span)])

    def holdings(first):
        blocks = {d: [d, mate(d, first)] for d in range(span)}
        last = blocks
        for step in range(1, rings):
            last = {d: last[mate(d, (first + step) % 2)] for d in range(span)}
            blocks = {d: blocks[d] + last[d] for d in range(span)}
        return blocks

    forward_tab, inverse_tab = dft_tables(length, modes)

    def rows_of(device):
        own = np.arange(device * owned, (device + 1) * owned)
        return np.concatenate([own, modes + own])

    def device_tables(device, order):
        here = slice(device * slab, (device + 1) * slab)
        rows = np.concatenate([rows_of(d) for d in order])
        return np.stack(
            [
                forward_tab[rows][:, here],
                inverse_tab[here][:, rows],
                inverse_tab[here][:, rows].T,
                forward_tab[rows][:, here].T,
            ]
        )

    tables = jnp.asarray(
        np.stack(
            [
                np.stack([device_tables(d, holdings(first)[d]) for first in range(2)])
                for d in range(span)
            ]
        )
    )[me]
    send_fields = [tables[first, :1] for first in range(2)]
    middle_tables = [tables[first, 1:3] for first in range(2)]
    take_back = [tables[first, 3:] for first in range(2)]

    token = jnp.zeros((8, lanes), full)

    def call(kernel, grid, ins, outs, shapes, scratch_shapes=(), aliases=()):
        near, far = len(ins), len(outs)

        def body(*refs):
            kernel(*refs[:near], *refs[near + 1 : near + 1 + far], *refs[near + 2 + far :])

        def run(*values):
            nonlocal token
            passed = pl.BlockSpec(memory_space=pl.ANY)
            *results, token = pl.pallas_call(
                body,
                grid=grid,
                in_specs=ins + [passed],
                out_specs=outs + [passed],
                out_shape=shapes + [jax.ShapeDtypeStruct(token.shape, token.dtype)],
                scratch_shapes=scratch_shapes,
                input_output_aliases=dict(aliases) | {near: far},
                cost_estimate=pl.CostEstimate(flops=1, bytes_accessed=1, transcendentals=0),
                compiler_params=pltpu.CompilerParams(vmem_limit_bytes=56 << 20),
            )(*values, token)
            return results

        return run

    def pin(value):
        nonlocal token
        value, token = lax.optimization_barrier((value, token))
        return value

    def whole(shape):
        return pl.BlockSpec(shape, lambda *_: (0,) * len(shape))

    def shape_of(*dims, kind=half):
        return jax.ShapeDtypeStruct(dims, kind)

    fields = features.reshape(slab, flat)
    cotan = cotangent.reshape(slab, flat)

    ahead, astern = [], []
    for first in range(2):
        other = jnp.asarray(np.array([mate(d, first) for d in range(span)], np.int32))[me]
        weight = jnp.concatenate(
            [lax.dynamic_slice_in_dim(spec_weight, d * owned, owned, 1) for d in (me, other)], 1
        )
        for result, matrix in ((ahead, weight.swapaxes(2, 3)), (astern, weight)):
            doubled = jnp.concatenate([twice(matrix[0]), twice(matrix[1])], -1)
            result.append(doubled.reshape(-1, 2 * lanes))
    skip_ahead, skip_back = twice(skip_weight.T), twice(skip_weight)
    in_ahead, in_back = twice(w_in), twice(w_in.T)
    out_ahead, out_back = twice(w_out), twice(w_out.T)

    def at(rows, c, size, first=0):
        return pl.BlockSpec((rows, size), lambda i: (0, starts[c] // size + first + i))

    def in_chunk(rows, size, first=0):
        return pl.BlockSpec((rows, size), lambda i: (0, first + i))

    pair = 2 * height
    def part_spec(c):
        return pl.BlockSpec((pair, counts[c]), lambda i: (0, 0))


    def partial_transform(c):
        return (
            call(
                partial_kernel,
                (counts[c] // broad,),
                [whole(send_fields[0].shape), at(slab, c, broad)],
                [in_chunk(pair, broad)] * rings,
                [shape_of(pair, counts[c])] * rings,
            )(send_fields[c % 2], fields)
        )

    def modal_forward(c, parts):
        return (
            call(
                functools.partial(modal_kernel, height),
                (1,),
                [whole(ahead[0].shape)] + [part_spec(c)] * len(parts),
                [part_spec(c)] * 2,
                [shape_of(pair, counts[c])] * 2,
            )(ahead[c % 2], *parts)
        )

    def modal_backward(c, spectrum, before, parts):
        return (
            call(
                functools.partial(modal_back_kernel, height),
                (1,),
                [whole(astern[0].shape), part_spec(c), whole(before.shape)] + [part_spec(c)] * len(parts),
                [part_spec(c), whole(before.shape)],
                [shape_of(pair, counts[c]), shape_of(*before.shape, kind=full)],
            )(astern[c % 2], spectrum, before, *parts)
        )

    def pointwise_part(c, number, modal, grads, buffers):
        steps = counts[c] // tile // cuts
        first = number * steps
        shapes = [shape_of(slab, flat), shape_of(slab, counts[c])]
        shapes += [shape_of(*grads.shape, kind=full)]
        shapes += [shape_of(pair, counts[c])] * rings
        base = 9 + rings
        spots = [0] + [1] * (number > 0) + list(range(3, 3 + rings)) * (number > 0)
        given = [buffers[spot] for spot in spots if buffers[spot] is not None]
        spots = [spot for spot in spots if buffers[spot] is not None]
        return (
            call(
                functools.partial(pointwise_kernel, rings, len(given)),
                (steps,),
                [
                    whole(middle_tables[0].shape),
                    at(slab, c, tile, first),
                    at(slab, c, tile, first),
                ]
                + [in_chunk(pair, tile, first)] * rings
                + [
                    whole(skip_ahead.shape),
                    whole(in_ahead.shape),
                    whole(out_ahead.shape),
                    whole(in_back.shape),
                    whole(out_back.shape),
                    whole(grads.shape),
                ]
                + [pl.BlockSpec(memory_space=pl.ANY)] * len(given),
                [
                    at(slab, c, tile, first),
                    in_chunk(slab, tile, first),
                    whole(grads.shape),
                ]
                + [in_chunk(pair, tile, first)] * rings,
                shapes,
                scratch_shapes=[
                    pltpu.VMEM((lanes, 2 * units), full),
                    pltpu.VMEM((lanes, 2 * units), full),
                    pltpu.VMEM((lanes, lanes), full),
                ],
                aliases={base + i: spot for i, spot in enumerate(spots)},
            )(
                middle_tables[c % 2],
                fields,
                cotan,
                *modal,
                skip_ahead,
                in_ahead,
                out_ahead,
                in_back,
                out_back,
                grads,
                *given,
            )
        )

    def final_chunk(c, grad_pre, parts, before):
        aliased = {} if before is None else {3: 0}
        if before is None:
            before = jnp.zeros((16, lanes), half)
        result = call(
            final_kernel,
            (counts[c] // broad,),
            [
                whole(take_back[0].shape),
                in_chunk(slab, broad),
                whole(skip_back.shape),
                pl.BlockSpec(memory_space=pl.ANY),
            ]
            + [in_chunk(pair, broad)] * rings,
            [at(slab, c, broad)],
            [shape_of(slab, flat)],
            aliases=aliased,
        )(take_back[c % 2], grad_pre, skip_back, before, *parts)
        return result[0]

    def add(left, right):
        return (left.astype(full) + right.astype(full)).astype(half)

    def beside(value, bit):
        return lax.ppermute(value, "dp", [(d, d ^ bit) for d in range(copies)])

    def summing(value):
        for i in range(copies.bit_length() - 1):
            value = pin(value + beside(value, 1 << i))
            yield value
        for i in range(span.bit_length() - 1):
            came = lax.ppermute(value, "space", [(d, d ^ (1 << i)) for d in range(span)])
            value = pin(value + came)
            yield value

    core = lax.axis_index("dp") % 2
    piece = owned // 2

    def collecting(value):
        kept = lax.dynamic_slice_in_dim(value, core * piece, piece, 1)
        given = lax.dynamic_slice_in_dim(value, (1 - core) * piece, piece, 1)
        kept = pin(kept + beside(given, 1))
        yield kept
        bit = 2
        while bit < copies:
            kept = pin(kept + beside(kept, bit))
            yield kept
            bit *= 2
        blocks = pin(jnp.stack([kept, swap(kept, 0)]))
        yield blocks
        held = [blocks]
        for step in range(1, rings):
            held.append(pin(swap(held[-1], step % 2)))
            yield held
        twins = [beside(value, 1) for value in held]
        order = jnp.asarray(np.array([holdings(0)[d] for d in range(span)], np.int32))[me]
        order = jnp.concatenate([order * 2 + core, order * 2 + 1 - core]).astype(jnp.int32)
        yield pl.pallas_call(
            place_kernel,
            in_specs=[pl.BlockSpec(memory_space=pltpu.SMEM)]
            + [pl.BlockSpec(memory_space=pltpu.VMEM)] * (2 * rings),
            out_specs=pl.BlockSpec(memory_space=pltpu.VMEM),
            out_shape=shape_of(2, modes, width, width, kind=full),
        )(order, *held, *twins)

    mixed = grad_fields = None
    grads = jnp.zeros((width, 2 * units + lanes), full)
    grad_spec = jnp.zeros((2, owned, width, width), full)
    parts, came, held, spectra, grad_pres = {}, {}, {}, {}, {}
    sums = pieces = None
    weights = 0
    spec_result = None
    for job in itertools.chain.from_iterable(jobs.split() for jobs in plan):
        kind, c = job[0].upper(), int(job[1:] or 0)
        turn = c % 2

        def swapped(value, step, turn=turn):
            return swap(value, (turn + step) % 2)

        if kind == "W":
            if weights == 0:
                ahead = pin(ahead)
            elif weights == 1:
                skip_ahead, in_ahead, in_back, out_ahead, out_back = pin(
                    (skip_ahead, in_ahead, in_back, out_ahead, out_back)
                )
            else:
                astern, skip_back = pin((astern, skip_back))
            weights += 1
        elif kind == "K":
            parts[c] = partial_transform(c)
            came[c] = swapped(parts[c][-1], rings - 1)
        elif kind in "AB":
            step = rings - (2 if kind == "A" else 3)
            total = pin(add(parts[c][step], came[c]))
            came[c] = swapped(total, step)
        elif kind == "C":
            total = pin(add(parts[c][0], came[c]))
            parts[c] = [parts[c][0], came[c], swapped(total, 0)]
        elif job[0] == "M":
            spectra[c], modal = modal_forward(c, parts[c])
            held[c] = [modal, swapped(modal, 1)]
        elif job[0] == "n":
            back, grad_spec = modal_backward(c, spectra[c], grad_spec, parts[c])
            held[c] = [back, swapped(back, 1)]
        elif kind in "EF":
            step = 2 if kind == "E" else 3
            last = pin(held[c][-1])
            held[c] = held[c][:-1] + [last, swapped(last, step)]
        elif kind == "P":
            number = int(job[0] == "p")
            buffers = [mixed, grad_pres.get(c), None] + list(parts[c] if number else [None] * rings)
            mixed, grad_pres[c], grads, *parts[c] = pointwise_part(
                c, number, held[c], grads, buffers
            )
            if number == cuts - 1:
                came[c] = swapped(parts[c][-1], rings - 1)
        elif kind == "Q":
            grad_fields = final_chunk(c, grad_pres[c], held[c], grad_fields)
        elif kind == "S":
            sums = summing(grads) if sums is None else sums
            grads = next(sums)
        else:
            pieces = collecting(grad_spec) if pieces is None else pieces
            spec_result = next(pieces)
    for grads in sums:
        pass
    for spec_result in pieces:
        pass
    grad_spec = spec_result
    grad_in = grads[:, :units]
    grad_out = grads[:, units : 2 * units].T
    grad_skip = grads[:, 2 * units : 2 * units + width]
    return (
        mixed.reshape(features.shape),
        grad_fields.reshape(features.shape),
        grad_spec,
        grad_skip,
        grad_in,
        grad_out,
    )


def shards(features, cotangent, spec_weight, skip_weight, w_in, w_out):
    span = lax.axis_size("space")
    copies = lax.axis_size("dp")
    batch, slab, flat = features.shape
    pairs = copies % 2 == 0 and (copies * span) & (copies * span - 1) == 0
    if batch == 1 and pairs and fits(span, slab, flat, w_in.shape[0], spec_weight.shape[1]):
        return slab_shards(features, cotangent, spec_weight, skip_weight, w_in, w_out)
    return pencil_shards(features, cotangent, spec_weight, skip_weight, w_in, w_out)


def solution(mesh):
    return jax.shard_map(
        shards,
        mesh=mesh,
        in_specs=(P("dp", "space", None), P("dp", "space", None), P(), P(), P(), P()),
        out_specs=(P("dp", "space", None), P("dp", "space", None), P(), P(), P(), P()),
        check_vma=False,
    )
```
